512 devices in a mesh: lat: 16 (over z, core), lon: 32 (over x, y).
Axes of the slice: x: 4, y: 8, z: 8, core: 2. Of those that a mesh axis runs over, the one named last changes fastest.
Arguments:
- fields: bfloat16 [512, 1024, 256], P('lat', 'lon'), may hold values from -6 to 6
- cotangent: bfloat16 [512, 1024, 256], P('lat', 'lon'), may hold values from -6 to 6
- mix_low: bfloat16 [32, 64, 256, 256], P('lat', 'lon'), may hold values from -6 to 6
- mix_high: bfloat16 [32, 64, 256, 256], P('lat', 'lon'), may hold values from -6 to 6
- point_weight: bfloat16 [256, 256], replicated, may hold values from -0.375 to 0.375
- point_bias: float32 [256], replicated, may hold values from -3 to 3
Outputs:
- field_grad: bfloat16 [512, 1024, 256], P('lat', 'lon')
- mix_low_grad: bfloat16 [32, 64, 256, 256], P('lat', 'lon')
- mix_high_grad: bfloat16 [32, 64, 256, 256], P('lat', 'lon')
- point_weight_grad: float32 [256, 256], replicated
- point_bias_grad: float32 [256], replicated
The draws below stay inside these ranges and needn't reach their ends.
All inputs are finite; a program needn't handle non-finite values.
Results may differ from the reference program's by a relative error of at most 0.0085.
Values sent between devices are 32-bit elements; how exact they have to be, the bound alone decides.
A program may use at most 64 MiB of HBM per device.

```python
import math
import jax
import jax.numpy as jnp
from jax import lax

C = 256
LEVELS = 4
NLAT = 512
NLON = 1024
KLAT = 32
KLON = 64


def block_levels(rng, extent, pieces, low, high):
    loudness = 1.0
    for dim, blocks in pieces:
        draws = jax.random.uniform(jax.random.fold_in(jax.random.fold_in(rng, 6), dim), (blocks,), jnp.float32, low / len(pieces), high / len(pieces))
        loudness = loudness * jnp.repeat(jnp.exp(draws), extent[dim] // blocks).reshape((-1,) + (1,) * (len(extent) - 1 - dim))
    return loudness


def scatter_about(rng, extent, scale, reach, shards=(), held_as=jnp.bfloat16):
    values = jax.random.normal(rng, extent, jnp.float32) * scale
    if len(shards) > 0:
        values = block_levels(rng, extent, shards, -0.22, 0.18) * values
    return jnp.clip(values, min=-reach, max=reach).astype(held_as)


def setup_inputs(seed: int = 0) -> dict:
    arg_keys = jax.random.split(jax.random.key(seed), 7)
    return {
        "fields": scatter_about(arg_keys[0], (NLAT, NLON, C), 1.0, 6.0, ((0, 16), (1, 32))),
        "cotangent": scatter_about(arg_keys[1], (NLAT, NLON, C), 1.0, 6.0, ((0, 16), (1, 32))),
        "mix_low": scatter_about(arg_keys[2], (KLAT, KLON, C, C), (max(1, C // 256)) ** -0.5, 6.0, ((0, 16), (1, 32))),
        "mix_high": scatter_about(arg_keys[3], (KLAT, KLON, C, C), (max(1, C // 256)) ** -0.5, 6.0, ((0, 16), (1, 32))),
        "point_weight": scatter_about(arg_keys[4], (C, C), C ** -0.5, 0.375),
        "point_bias": scatter_about(arg_keys[5], (C,), 0.5, 3.0, (), jnp.float32),
    }


low_taps = (-0.010597401784997278, 0.032883011666982945, 0.030841381835986965, -0.18703481171888114, -0.02798376941698385, 0.6308807679295904, 0.7148465705525415, 0.23037781330885523)
high_taps = (-0.23037781330885523, 0.7148465705525415, -0.6308807679295904, -0.02798376941698385, 0.18703481171888114, 0.030841381835986965, -0.032883011666982945, -0.010597401784997278)

def filter_down(field_in, filter_taps, dim_index, pad_mode):
    count_in = field_in.shape[dim_index]
    widths = [(0, 0), (0, 0), (0, 0)]
    widths[dim_index] = (3, 4)
    padded = jnp.pad(field_in, widths, mode=pad_mode)
    result = filter_taps[0] * lax.slice_in_dim(padded, 0, count_in, 2, dim_index)
    for tap_index in range(1, 8):
        result = result + filter_taps[tap_index] * lax.slice_in_dim(padded, tap_index, tap_index + count_in, 2, dim_index)
    return result

def filter_up(coefficients, filter_taps, dim_index, pad_mode):
    count_in = coefficients.shape[dim_index]
    widths = [(0, 0), (0, 0), (0, 0)]
    widths[dim_index] = (2, 2)
    padded = jnp.pad(coefficients, widths, mode=pad_mode)
    even_part = filter_taps[1] * lax.slice_in_dim(padded, 3, 3 + count_in, 1, dim_index)
    odd_part = filter_taps[0] * lax.slice_in_dim(padded, 4, 4 + count_in, 1, dim_index)
    for position in range(1, 4):
        even_part = even_part + filter_taps[2 * position + 1] * lax.slice_in_dim(padded, 3 - position, 3 - position + count_in, 1, dim_index)
        odd_part = odd_part + filter_taps[2 * position] * lax.slice_in_dim(padded, 4 - position, 4 - position + count_in, 1, dim_index)
    stacked = jnp.stack([even_part, odd_part], dim_index + 1)
    new_shape = list(even_part.shape)
    new_shape[dim_index] = 2 * count_in
    return stacked.reshape(new_shape)

def analyse(source):
    approx = source
    for level_index in range(LEVELS - 1):
        approx = filter_down(filter_down(approx, low_taps, 0, 'constant'), low_taps, 1, 'wrap')
    across = filter_down(approx, low_taps, 0, 'constant')
    return (filter_down(across, low_taps, 1, 'wrap'), filter_down(across, high_taps, 1, 'wrap'))

def synthesise(low_coef, high_coef):
    widened = filter_up(low_coef, low_taps, 1, 'wrap') + filter_up(high_coef, high_taps, 1, 'wrap')
    approx = filter_up(widened, low_taps, 0, 'constant')
    for level_index in range(LEVELS - 1):
        approx = filter_up(filter_up(approx, low_taps, 1, 'wrap'), low_taps, 0, 'constant')
    return approx

def reference(fields, cotangent, mix_low, mix_high, point_weight, point_bias):
    channels = fields.shape[2]
    source = fields.astype(jnp.float32)
    low_coef, high_coef = analyse(source)
    low_rounded = low_coef.astype(jnp.bfloat16)
    high_rounded = high_coef.astype(jnp.bfloat16)
    mixed_low = jnp.einsum('pqi,pqio->pqo', low_rounded.astype(jnp.float32), mix_low.astype(jnp.float32))
    mixed_high = jnp.einsum('pqi,pqio->pqo', high_rounded.astype(jnp.float32), mix_high.astype(jnp.float32))
    spectral = synthesise(mixed_low, mixed_high)
    flat_fields = fields.reshape(NLAT * NLON, channels)
    pointwise = jnp.dot(flat_fields, point_weight, preferred_element_type=jnp.float32) + point_bias
    preact = spectral + pointwise.reshape(NLAT, NLON, channels)
    normal_cdf = 0.5 * (1.0 + lax.erf(preact * (1.0 / math.sqrt(2.0))))
    normal_pdf = jnp.exp(-0.5 * preact * preact) * (1.0 / math.sqrt(2.0 * math.pi))
    grad_pre = cotangent.astype(jnp.float32) * (normal_cdf + preact * normal_pdf)
    grad_rounded = grad_pre.astype(jnp.bfloat16)
    flat_grad = grad_rounded.reshape(NLAT * NLON, channels)
    grad_scale = 1.0 / math.sqrt(NLAT * NLON)
    weight_total = lax.dot_general(flat_fields, flat_grad, (((0,), (0,)), ((), ())), preferred_element_type=jnp.float32)
    bias_total = lax.optimization_barrier(jnp.sum(grad_pre, axis=(0, 1)))
    back_low, back_high = analyse(grad_pre)
    mix_low_grad = (low_rounded.astype(jnp.float32)[:, :, :, None] * back_low[:, :, None, :]).astype(jnp.bfloat16)
    mix_high_grad = (high_rounded.astype(jnp.float32)[:, :, :, None] * back_high[:, :, None, :]).astype(jnp.bfloat16)
    pull_low = jnp.einsum('pqo,pqio->pqi', back_low.astype(jnp.bfloat16).astype(jnp.float32), mix_low.astype(jnp.float32))
    pull_high = jnp.einsum('pqo,pqio->pqi', back_high.astype(jnp.bfloat16).astype(jnp.float32), mix_high.astype(jnp.float32))
    pulled = synthesise(pull_low, pull_high)
    direct = lax.dot_general(flat_grad, point_weight, (((1,), (1,)), ((), ())), preferred_element_type=jnp.float32)
    field_grad = (pulled + direct.reshape(NLAT, NLON, channels)).astype(jnp.bfloat16)
    return (field_grad, mix_low_grad, mix_high_grad, weight_total * grad_scale, bias_total * grad_scale)
```

```python
import functools
import math

import jax
import jax.numpy as jnp
import numpy as np
from jax import lax
from jax.experimental import pallas as pl
from jax.experimental.pallas import tpu as pltpu
from jax.sharding import PartitionSpec as P

MESH = pl.DeviceIdType.MESH
F32 = jnp.float32
BF16 = jnp.bfloat16
ROW = 8

low_taps = (
    -0.010597401784997278,
    0.032883011666982945,
    0.030841381835986965,
    -0.18703481171888114,
    -0.02798376941698385,
    0.6308807679295904,
    0.7148465705525415,
    0.23037781330885523,
)
high_taps = (
    -0.23037781330885523,
    0.7148465705525415,
    -0.6308807679295904,
    -0.02798376941698385,
    0.18703481171888114,
    0.030841381835986965,
    -0.032883011666982945,
    -0.010597401784997278,
)


def level_matrix(count, taps, closed):
    matrix = np.zeros((count // 2, count))
    for k in range(count // 2):
        for j in range(8):
            n = 2 * k + j - 3
            if closed:
                matrix[k, n % count] += taps[j]
            elif 0 <= n < count:
                matrix[k, n] += taps[j]
    return matrix


def analysis_matrix(count, last_taps, closed):
    product = level_matrix(count, low_taps, closed)
    for level in (1, 2):
        product = level_matrix(count >> level, low_taps, closed) @ product
    return level_matrix(count >> 3, last_taps, closed) @ product


def coarse_offset(block, half):
    if block < 3:
        return 2 * (block - 1) + half
    return -3 if half == 1 else 4


def band_tables(nlat, nlon, band, sector):
    lat = analysis_matrix(nlat, low_taps, False)
    lons = [analysis_matrix(nlon, taps, True) for taps in (low_taps, high_taps)]
    bands = nlat // band
    tables = []
    for d in (0, bands // 2, bands - 1):
        rows = np.zeros((4, 2, band))
        for block in range(4):
            for p in range(2):
                k = 2 * d + coarse_offset(block, p)
                if 0 <= k < lat.shape[0]:
                    rows[block, p] = lat[k, d * band : (d + 1) * band]
        cols = np.zeros((4, 2, 2, sector))
        for block in range(4):
            for q in range(2):
                k = (2 + coarse_offset(block, q)) % lons[0].shape[0]
                for f in range(2):
                    cols[block, q, f] = lons[f][k, sector : 2 * sector]
        table = np.einsum("apn,bqfm->abpqfnm", rows, cols)
        tables.append(table.reshape(128, band * sector))
    full = np.stack(tables).astype(np.float32)
    high = full.astype(jnp.bfloat16)
    low = (full - high.astype(np.float32)).astype(jnp.bfloat16)
    return np.concatenate([high, low], axis=1)


def kernel(
    dims, x_hbm, cot_hbm, mixl_hbm, mixh_hbm, w_hbm, bias_hbm, k_hbm,
    fg_hbm, mlg_hbm, mhg_hbm, wg_hbm, bg_hbm,
    x_v, cot_v, mixl_v, mixh_v, w_v, bias_v, kd_v,
    ku_v, xt_v, wt_v, ghi_v, glo_v, mm_v, ml_v, bacc_v,
    fg_v, mlg_v, mhg_v, wg_v, bg_v,
    as_v, ar_v, ss_v, sr_v, gm_v, gr_v, gs_v, gg_v,
    cs_v, cr_v, xs_v, xr_v, zs_v, zr_v, ys_v, yr_v, af_v,
    in_sem, out_sem, h_send, h_recv, r_send, r_recv,
):
    nlat, nlon, ncells = dims
    nz, ny = nlat // 2, min(ROW, nlon // 2)
    nx = nlon // ny
    tx = 32 // nx
    tz = tx // nz
    lat, lon = lax.axis_index("lat"), lax.axis_index("lon")
    core, z = lax.rem(lat, 2), lat // 2
    y, x = lax.rem(lon, ny), lon // ny

    def at_lat(step):
        return {"lat": lax.rem(lat + step + nlat, nlat)}

    def at_lon(step):
        return {"lon": lax.rem(lon + step + nlon, nlon)}

    partner = {"lat": lat + 1 - 2 * core}

    def at_z(k):
        return lax.rem(z + k, nz)

    def at_x(k):
        return lax.rem(x + k, nx)

    def at_y(k):
        return lax.rem(y + k, ny)

    variant = (lat + nlat - 2) // (nlat - 1) + lat // (nlat - 1)
    loads = [
        (x_hbm, x_v), (k_hbm.at[variant], kd_v), (w_hbm, w_v), (bias_hbm, bias_v),
        (mixl_hbm, mixl_v), (mixh_hbm, mixh_v), (cot_hbm, cot_v),
    ]
    loads = [pltpu.make_async_copy(s, d, in_sem.at[i]) for i, (s, d) in enumerate(loads)]
    for copy in loads:
        copy.start()

    barrier = pltpu.get_barrier_semaphore()
    near = [at_lat(1), at_lat(-1), at_lon(1), at_lon(-1), at_lon(2), at_lon(-2)]
    near += [{"lat": at_z(k) * 2 + core} for k in range(1, nz)]
    near += [{"lon": at_x(k) * ny + y} for k in range(1, nx)]
    near += [{"lon": x * ny + at_y(k)} for k in range(1, ny)]
    for device in near:
        pl.semaphore_signal(barrier, inc=1, device_id=device, device_id_type=MESH)

    sends = []

    def push(src, dst, send_sem, recv_sem, device):
        copy = pltpu.make_async_remote_copy(
            src_ref=src, dst_ref=dst, send_sem=send_sem, recv_sem=recv_sem,
            device_id=device, device_id_type=MESH,
        )
        copy.start()
        sends.append(copy)
        return copy

    row = lax.broadcasted_iota(jnp.int32, (8, 256), 0)
    lower_p = row < 4
    lower_q = lax.rem(row // 2, 2) < 1
    below = jnp.where(lat >= 2, 1.0, 0.0)
    above = jnp.where(lat + 2 < nlat, 1.0, 0.0)

    def partial_lat_start(e, hi, lo):
        if lo is None:
            whole = jnp.dot(kd_v[...], hi, preferred_element_type=F32)
            part = whole[:128] + whole[128:]
        else:
            whole = jnp.dot(kd_v[...], hi, preferred_element_type=F32)
            part = whole[:128] + whole[128:]
            part = part + jnp.dot(kd_v[:128], lo, preferred_element_type=F32)
        as_v[e] = part.reshape(4, 4, 8, 256)

    def partial_lat_send(e):
        plan = ((0, 0, -1), (2, 1, 1), (3, 2, -2), (3, 3, 2))
        return [
            push(as_v.at[e, block], ar_v.at[e, slot], h_send.at[e, 0, slot],
                 h_recv.at[e, 0, slot], at_lat(step))
            for block, slot, step in plan
        ]

    def partial_lon(e, copies):
        for copy in copies:
            copy.wait_recv()
        for tile in range(4):
            far = jnp.where(lower_p, ar_v[e, 3, tile] * below, ar_v[e, 2, tile] * above)
            ss_v[e, tile] = (as_v[e, 1, tile] + ar_v[e, 0, tile]) + (ar_v[e, 1, tile] + far)
        plan = ((0, 0, -1), (2, 1, 1), (3, 2, -2), (3, 3, 2))
        return [
            push(ss_v.at[e, tile], sr_v.at[e, slot], h_send.at[e, 1, slot],
                 h_recv.at[e, 1, slot], at_lon(step))
            for tile, slot, step in plan
        ]

    def partial_done(e, copies):
        for copy in copies:
            copy.wait_recv()
        far = jnp.where(lower_q, sr_v[e, 3], sr_v[e, 2])
        return (ss_v[e, 1] + sr_v[e, 0]) + (sr_v[e, 1] + far)

    def spread_lon(e, tile):
        gm_v[e] = tile
        plan = ((0, 1), (1, -1), (2, 2), (3, -2))
        return [
            push(gm_v.at[e], gr_v.at[e, slot], h_send.at[e, 2, slot],
                 h_recv.at[e, 2, slot], at_lon(step))
            for slot, step in plan
        ]

    def spread_lat(e, copies):
        for copy in copies:
            copy.wait_recv()
        gs_v[e, 0] = gr_v[e, 0]
        gs_v[e, 1] = gm_v[e]
        gs_v[e, 2] = gr_v[e, 1]
        gs_v[e, 3] = jnp.where(lower_q, gr_v[e, 3], gr_v[e, 2])
        plan = ((0, 1), (1, -1), (2, 2), (3, -2))
        return [
            push(gs_v.at[e], gg_v.at[e, slot], h_send.at[e, 3, slot],
                 h_recv.at[e, 3, slot], at_lat(step))
            for slot, step in plan
        ]

    def spread_done(e, copies):
        for copy in copies:
            copy.wait_recv()
        far = jnp.where(lower_p[None], gg_v[e, 3] * above, gg_v[e, 2] * below)
        parts = (gg_v[e, 0], gs_v[e], gg_v[e, 1], far)
        for block, part in enumerate(parts):
            part = part.reshape(32, 256)
            high = part.astype(BF16)
            low = (part - high.astype(F32)).astype(BF16)
            mm_v[pl.ds(32 * block, 32), :] = high
            mm_v[pl.ds(128 + 32 * block, 32), :] = high
            ml_v[pl.ds(32 * block, 32), :] = low

    def picked(tile, r):
        return jnp.where(row == r, tile, 0.0).astype(BF16)

    def mixer(r):
        p, q, f = r // 4, (r // 2) % 2, r % 2
        return (mixh_v if f else mixl_v)[p, q]

    loads[0].wait()
    loads[1].wait()
    partial_lat_start(0, x_v[...], None)
    pl.semaphore_wait(barrier, len(near))
    copies = partial_lat_send(0)

    loads[2].wait()
    loads[3].wait()
    ku_v[...] = kd_v[...].T
    xt_v[...] = x_v[...].T
    wt_v[...] = w_v[...].T
    loads[4].wait()
    loads[5].wait()
    loads[6].wait()

    copies = partial_lon(0, copies)
    coarse = partial_done(0, copies).astype(BF16).astype(F32)
    mixed = jnp.dot(picked(coarse, 0), mixer(0), preferred_element_type=F32)
    for r in range(1, 8):
        mixed = mixed + jnp.dot(picked(coarse, r), mixer(r), preferred_element_type=F32)
    copies = spread_lon(0, mixed)
    copies = spread_lat(0, copies)
    spread_done(0, copies)

    bacc_v[...] = jnp.zeros_like(bacc_v)
    chunk = 256

    def gate(i, carry):
        rows = pl.ds(pl.multiple_of(i * chunk, chunk), chunk)
        pre = jnp.dot(ku_v[rows, :], mm_v[...], preferred_element_type=F32)
        pre = pre + jnp.dot(ku_v[rows, :128], ml_v[...], preferred_element_type=F32)
        pre = pre + jnp.dot(x_v[rows, :], w_v[...], preferred_element_type=F32)
        pre = pre + bias_v[...]
        cdf = 0.5 * (1.0 + lax.erf(pre * (1.0 / math.sqrt(2.0))))
        pdf = jnp.exp(-0.5 * pre * pre) * (1.0 / math.sqrt(2.0 * math.pi))
        grad = cot_v[rows, :].astype(F32) * (cdf + pre * pdf)
        high = grad.astype(BF16)
        ghi_v[rows, :] = high
        glo_v[rows, :] = (grad - high.astype(F32)).astype(BF16)
        bacc_v[...] += jnp.sum(grad.reshape(chunk // 8, 8, 256), axis=0)
        return carry

    lax.fori_loop(0, 1024 // chunk, gate, 0)

    total = jnp.dot(xt_v[...], ghi_v[...], preferred_element_type=F32)
    bias_sum = jnp.sum(bacc_v[...], axis=0, keepdims=True)
    row1 = lax.broadcasted_iota(jnp.int32, (8, 128), 0)
    bias_tile = jnp.where(row1 == 0, bias_sum[:, :128], 0.0)
    bias_tile = jnp.where(row1 == 1, bias_sum[:, 128:], bias_tile)
    for h in range(2):
        cs_v[h, :32] = total[:, h * 128 : (h + 1) * 128].reshape(32, 8, 128)
        cs_v[h, 32] = bias_tile
    sem = iter(range(64))
    k = next(sem)
    core_copy = push(cs_v.at[1 - core], cr_v, r_send.at[k], r_recv.at[k], partner)

    partial_lat_start(1, ghi_v[...], glo_v[...])
    copies = partial_lat_send(1)

    core_copy.wait_recv()
    red = cs_v[core, :32] + cr_v[:32]
    red_bias = cs_v[core, 32] + cr_v[32]
    for j in range(nx):
        xs_v[j, :tx] = red[j * tx : (j + 1) * tx]
        xs_v[j, tx] = red_bias
    xr_v[x] = xs_v[x]
    x_copies = []
    for j in range(1, nx):
        k = next(sem)
        x_copies.append(push(xs_v.at[at_x(j)], xr_v.at[x], r_send.at[k], r_recv.at[k],
                             {"lon": at_x(j) * ny + y}))

    copies = partial_lon(1, copies)

    for copy in x_copies:
        copy.wait_recv()
    red = xr_v[0]
    for j in range(1, nx):
        red = red + xr_v[j]
    for j in range(nz):
        zs_v[j, :tz] = red[j * tz : (j + 1) * tz]
        zs_v[j, tz] = red[tx]
    zr_v[z] = zs_v[z]
    z_copies = []
    for j in range(1, nz):
        k = next(sem)
        z_copies.append(push(zs_v.at[at_z(j)], zr_v.at[z], r_send.at[k], r_recv.at[k],
                             {"lat": at_z(j) * 2 + core}))

    back = partial_done(1, copies)
    back_rounded = back.astype(BF16).astype(F32)
    pull = None
    for r in range(8):
        term = lax.dot_general(picked(back_rounded, r), mixer(r), (((1,), (1,)), ((), ())),
                               preferred_element_type=F32)
        pull = term if pull is None else pull + term
    copies = spread_lon(1, pull)

    for copy in z_copies:
        copy.wait_recv()
    red = zr_v[0]
    for j in range(1, nz):
        red = red + zr_v[j]
    ys_v[...] = red
    yr_v[y] = red
    y_copies = []
    for j in range(1, ny):
        k = next(sem)
        y_copies.append(push(ys_v, yr_v.at[y], r_send.at[k], r_recv.at[k],
                             {"lon": x * ny + at_y(j)}))

    copies = spread_lat(1, copies)

    columns = coarse.T
    for r in range(8):
        p, q, f = r // 4, (r // 2) % 2, r % 2
        outer = (columns[:, r : r + 1] * back[r : r + 1, :]).astype(BF16)
        (mhg_v if f else mlg_v)[p, q] = outer
    outs = [pltpu.make_async_copy(mlg_v, mlg_hbm, out_sem.at[0]),
            pltpu.make_async_copy(mhg_v, mhg_hbm, out_sem.at[1])]
    for copy in outs:
        copy.start()

    for copy in y_copies:
        copy.wait_recv()
    red = yr_v[0]
    for j in range(1, ny):
        red = red + yr_v[j]
    red = red * (1.0 / math.sqrt(ncells))
    af_v[core, x, z] = red[:tz]
    z_copies = []
    for j in range(1, nz):
        k = next(sem)
        z_copies.append(push(af_v.at[core, x, z], af_v.at[core, x, z], r_send.at[k], r_recv.at[k],
                             {"lat": at_z(j) * 2 + core}))
    bg_v[:, :128] = red[tz][0:1, :]
    bg_v[:, 128:] = red[tz][1:2, :]

    spread_done(1, copies)

    def back_out(i, carry):
        rows = pl.ds(pl.multiple_of(i * chunk, chunk), chunk)
        out = jnp.dot(ku_v[rows, :], mm_v[...], preferred_element_type=F32)
        out = out + jnp.dot(ku_v[rows, :128], ml_v[...], preferred_element_type=F32)
        out = out + jnp.dot(ghi_v[rows, :], wt_v[...], preferred_element_type=F32)
        fg_v[rows, :] = out.astype(BF16)
        return carry

    lax.fori_loop(0, 1024 // chunk, back_out, 0)
    outs.append(pltpu.make_async_copy(fg_v, fg_hbm, out_sem.at[2]))
    outs[-1].start()

    for copy in z_copies:
        copy.wait_recv()
    x_copies = []
    for j in range(1, nx):
        k = next(sem)
        x_copies.append(push(af_v.at[core, x], af_v.at[core, x], r_send.at[k], r_recv.at[k],
                             {"lon": at_x(j) * ny + y}))
    for copy in x_copies:
        copy.wait_recv()
    k = next(sem)
    core_copy = push(af_v.at[core], af_v.at[core], r_send.at[k], r_recv.at[k], partner)
    core_copy.wait_recv()
    for h in range(2):
        wg_v[:, h * 128 : (h + 1) * 128] = af_v[h].reshape(256, 128)
    outs.append(pltpu.make_async_copy(wg_v, wg_hbm, out_sem.at[3]))
    outs.append(pltpu.make_async_copy(bg_v, bg_hbm, out_sem.at[4]))
    for copy in outs[3:]:
        copy.start()
    for copy in outs:
        copy.wait()
    for copy in sends:
        copy.wait_send()


def shards(fields, cotangent, mix_low, mix_high, point_weight, point_bias):
    nlat, nlon = lax.axis_size("lat"), lax.axis_size("lon")
    rows, cols, channels = fields.shape
    cells = rows * cols
    tables = jnp.asarray(band_tables(rows * nlat, cols * nlon, rows, cols))
    nz, ny = nlat // 2, min(ROW, nlon // 2)
    nx = nlon // ny
    tx = 32 // nx
    tz = tx // nz
    messages = 2 + 2 * (nx - 1) + 2 * (nz - 1) + (ny - 1)
    vmem = pltpu.VMEM
    scratch = [
        vmem((cells, channels), BF16), vmem((cells, channels), BF16),
        vmem(mix_low.shape, BF16), vmem(mix_high.shape, BF16),
        vmem((channels, channels), BF16), vmem((1, channels), F32), vmem((256, cells), BF16),
        vmem((cells, 256), BF16), vmem((channels, cells), BF16), vmem((channels, channels), BF16),
        vmem((cells, channels), BF16), vmem((cells, channels), BF16),
        vmem((256, channels), BF16), vmem((128, channels), BF16), vmem((8, channels), F32),
        vmem((cells, channels), BF16), vmem(mix_low.shape, BF16), vmem(mix_high.shape, BF16),
        vmem((channels, channels), F32), vmem((1, channels), F32),
        vmem((2, 4, 4, 8, channels), F32), vmem((2, 4, 4, 8, channels), F32),
        vmem((2, 4, 8, channels), F32), vmem((2, 4, 8, channels), F32),
        vmem((2, 8, channels), F32), vmem((2, 4, 8, channels), F32),
        vmem((2, 4, 8, channels), F32), vmem((2, 4, 4, 8, channels), F32),
        vmem((2, 33, 8, 128), F32), vmem((33, 8, 128), F32),
        vmem((nx, tx + 1, 8, 128), F32), vmem((nx, tx + 1, 8, 128), F32),
        vmem((nz, tz + 1, 8, 128), F32), vmem((nz, tz + 1, 8, 128), F32),
        vmem((tz + 1, 8, 128), F32), vmem((ny, tz + 1, 8, 128), F32),
        vmem((2, nx, nz, tz, 8, 128), F32),
        pltpu.SemaphoreType.DMA((7,)), pltpu.SemaphoreType.DMA((5,)),
        pltpu.SemaphoreType.DMA((2, 4, 4)), pltpu.SemaphoreType.DMA((2, 4, 4)),
        pltpu.SemaphoreType.DMA((messages,)), pltpu.SemaphoreType.DMA((messages,)),
    ]
    outs = pl.pallas_call(
        functools.partial(kernel, (nlat, nlon, cells * nlat * nlon)),
        out_shape=(
            jax.ShapeDtypeStruct((cells, channels), BF16),
            jax.ShapeDtypeStruct(mix_low.shape, BF16),
            jax.ShapeDtypeStruct(mix_high.shape, BF16),
            jax.ShapeDtypeStruct((channels, channels), F32),
            jax.ShapeDtypeStruct((1, channels), F32),
        ),
        in_specs=[pl.BlockSpec(memory_space=pl.ANY)] * 7,
        out_specs=[pl.BlockSpec(memory_space=pl.ANY)] * 5,
        scratch_shapes=scratch,
        compiler_params=pltpu.CompilerParams(
            collective_id=0, has_side_effects=True, vmem_limit_bytes=32 * 1024 * 1024
        ),
        name="wavelet_block",
    )(
        fields.reshape(cells, channels), cotangent.reshape(cells, channels), mix_low, mix_high,
        point_weight, point_bias.reshape(1, channels), tables,
    )
    return (
        outs[0].reshape(fields.shape), outs[1], outs[2], outs[3], outs[4].reshape(channels),
    )


def solution(mesh):
    placed = (
        P("lat", "lon", None),
        P("lat", "lon", None),
        P("lat", "lon", None, None),
        P("lat", "lon", None, None),
        P(),
        P(),
    )
    return jax.shard_map(
        shards,
        mesh=mesh,
        in_specs=placed,
        out_specs=(
            P("lat", "lon", None),
            P("lat", "lon", None, None),
            P("lat", "lon", None, None),
            P(),
            P(),
        ),
        check_vma=False,
    )
```

```python
import functools
import math

import jax
import jax.numpy as jnp
import numpy as np
from jax import lax
from jax.experimental import pallas as pl
from jax.experimental.pallas import tpu as pltpu
from jax.sharding import PartitionSpec as P

MESH = pl.DeviceIdType.MESH
F32 = jnp.float32
BF16 = jnp.bfloat16
ROW = 8

low_taps = (
    -0.010597401784997278,
    0.032883011666982945,
    0.030841381835986965,
    -0.18703481171888114,
    -0.02798376941698385,
    0.6308807679295904,
    0.7148465705525415,
    0.23037781330885523,
)
high_taps = (
    -0.23037781330885523,
    0.7148465705525415,
    -0.6308807679295904,
    -0.02798376941698385,
    0.18703481171888114,
    0.030841381835986965,
    -0.032883011666982945,
    -0.010597401784997278,
)


def level_matrix(count, taps, closed):
    matrix = np.zeros((count // 2, count))
    for k in range(count // 2):
        for j in range(8):
            n = 2 * k + j - 3
            if closed:
                matrix[k, n % count] += taps[j]
            elif 0 <= n < count:
                matrix[k, n] += taps[j]
    return matrix


def analysis_matrix(count, last_taps, closed):
    product = level_matrix(count, low_taps, closed)
    for level in (1, 2):
        product = level_matrix(count >> level, low_taps, closed) @ product
    return level_matrix(count >> 3, last_taps, closed) @ product


def coarse_offset(block, half):
    if block < 3:
        return 2 * (block - 1) + half
    return -3 if half == 1 else 4


def band_tables(nlat, nlon, band, sector):
    lat = analysis_matrix(nlat, low_taps, False)
    lons = [analysis_matrix(nlon, taps, True) for taps in (low_taps, high_taps)]
    bands = nlat // band
    tables = []
    for d in (0, bands // 2, bands - 1):
        rows = np.zeros((4, 2, band))
        for block in range(4):
            for p in range(2):
                k = 2 * d + coarse_offset(block, p)
                if 0 <= k < lat.shape[0]:
                    rows[block, p] = lat[k, d * band : (d + 1) * band]
        cols = np.zeros((4, 2, 2, sector))
        for block in range(4):
            for q in range(2):
                k = (2 + coarse_offset(block, q)) % lons[0].shape[0]
                for f in range(2):
                    cols[block, q, f] = lons[f][k, sector : 2 * sector]
        table = np.einsum("apn,bqfm->abpqfnm", rows, cols)
        tables.append(table.reshape(128, band * sector))
    full = np.stack(tables).astype(np.float32)
    high = full.astype(jnp.bfloat16)
    low = (full - high.astype(np.float32)).astype(jnp.bfloat16)
    return np.concatenate([high, low], axis=1)


def kernel(
    dims, x_hbm, cot_hbm, mixl_hbm, mixh_hbm, w_hbm, bias_hbm, k_hbm,
    fg_v, mlg_v, mhg_v, af_v, bg_v,
    x_v, cot_v, mixl_v, mixh_v, w_v, bias_v, kd_v,
    ku_v, xt_v, wt_v, ghi_v, glo_v, mm_v, ml_v, bacc_v,
    as_v, ar_v, ss_v, sr_v, gm_v, gr_v, gs_v, gg_v,
    cs_v, cr_v, xs_v, xr_v, zs_v, zr_v, ys_v, yr_v,
    bs_v, bc_v, br_v,
    in_sem, h_send, h_recv, r_send, r_recv,
):
    nlat, nlon, ncells = dims
    nz, ny = nlat // 2, min(ROW, nlon // 2)
    nx = nlon // ny
    tx = 32 // nx
    tz = tx // nz
    lat, lon = lax.axis_index("lat"), lax.axis_index("lon")
    core, z = lax.rem(lat, 2), lat // 2
    y, x = lax.rem(lon, ny), lon // ny

    def at_lat(step):
        return {"lat": lax.rem(lat + step + nlat, nlat)}

    def at_lon(step):
        return {"lon": lax.rem(lon + step + nlon, nlon)}

    partner = {"lat": lat + 1 - 2 * core}

    def at_z(k):
        return lax.rem(z + k, nz)

    def at_x(k):
        return lax.rem(x + k, nx)

    def at_y(k):
        return lax.rem(y + k, ny)

    variant = (lat + nlat - 2) // (nlat - 1) + lat // (nlat - 1)
    loads = [
        (x_hbm, x_v), (k_hbm.at[variant], kd_v), (w_hbm, w_v), (bias_hbm, bias_v),
        (mixl_hbm, mixl_v), (mixh_hbm, mixh_v), (cot_hbm, cot_v),
    ]
    loads = [pltpu.make_async_copy(s, d, in_sem.at[i]) for i, (s, d) in enumerate(loads)]
    for copy in loads:
        copy.start()

    barrier = pltpu.get_barrier_semaphore()
    near = [at_lat(1), at_lat(-1), at_lon(1), at_lon(-1), at_lon(2), at_lon(-2)]
    near += [{"lat": at_z(k) * 2 + core} for k in range(1, nz)]
    near += [{"lon": at_x(k) * ny + y} for k in range(1, nx)]
    near += [{"lon": x * ny + at_y(k)} for k in range(1, ny)]
    for device in near:
        pl.semaphore_signal(barrier, inc=1, device_id=device, device_id_type=MESH)

    sends = []

    def push(src, dst, send_sem, recv_sem, device):
        copy = pltpu.make_async_remote_copy(
            src_ref=src, dst_ref=dst, send_sem=send_sem, recv_sem=recv_sem,
            device_id=device, device_id_type=MESH,
        )
        copy.start()
        sends.append(copy)
        return copy

    row = lax.broadcasted_iota(jnp.int32, (8, 256), 0)
    lower_p = row < 4
    lower_q = lax.rem(row // 2, 2) < 1
    below = jnp.where(lat >= 2, 1.0, 0.0)
    above = jnp.where(lat + 2 < nlat, 1.0, 0.0)

    def partial_lat_start(e, hi, lo):
        if lo is None:
            whole = jnp.dot(kd_v[...], hi, preferred_element_type=F32)
            part = whole[:128] + whole[128:]
        else:
            whole = jnp.dot(kd_v[...], hi, preferred_element_type=F32)
            part = whole[:128] + whole[128:]
            part = part + jnp.dot(kd_v[:128], lo, preferred_element_type=F32)
        as_v[e] = part.reshape(4, 4, 8, 256)

    def partial_lat_send(e):
        plan = ((0, 0, -1), (2, 1, 1), (3, 2, -2), (3, 3, 2))
        return [
            push(as_v.at[e, block], ar_v.at[e, slot], h_send.at[e, 0, slot],
                 h_recv.at[e, 0, slot], at_lat(step))
            for block, slot, step in plan
        ]

    def partial_lon(e, copies):
        for copy in copies:
            copy.wait_recv()
        for tile in range(4):
            far = jnp.where(lower_p, ar_v[e, 3, tile] * below, ar_v[e, 2, tile] * above)
            ss_v[e, tile] = (as_v[e, 1, tile] + ar_v[e, 0, tile]) + (ar_v[e, 1, tile] + far)
        plan = ((0, 0, -1), (2, 1, 1), (3, 2, -2), (3, 3, 2))
        return [
            push(ss_v.at[e, tile], sr_v.at[e, slot], h_send.at[e, 1, slot],
                 h_recv.at[e, 1, slot], at_lon(step))
            for tile, slot, step in plan
        ]

    def partial_done(e, copies):
        for copy in copies:
            copy.wait_recv()
        far = jnp.where(lower_q, sr_v[e, 3], sr_v[e, 2])
        return (ss_v[e, 1] + sr_v[e, 0]) + (sr_v[e, 1] + far)

    def spread_lon(e, tile):
        gm_v[e] = tile
        plan = ((0, 1), (1, -1), (2, 2), (3, -2))
        return [
            push(gm_v.at[e], gr_v.at[e, slot], h_send.at[e, 2, slot],
                 h_recv.at[e, 2, slot], at_lon(step))
            for slot, step in plan
        ]

    def spread_lat(e, copies):
        for copy in copies:
            copy.wait_recv()
        gs_v[e, 0] = gr_v[e, 0]
        gs_v[e, 1] = gm_v[e]
        gs_v[e, 2] = gr_v[e, 1]
        gs_v[e, 3] = jnp.where(lower_q, gr_v[e, 3], gr_v[e, 2])
        plan = ((0, 1), (1, -1), (2, 2), (3, -2))
        return [
            push(gs_v.at[e], gg_v.at[e, slot], h_send.at[e, 3, slot],
                 h_recv.at[e, 3, slot], at_lat(step))
            for slot, step in plan
        ]

    def spread_done(e, copies):
        for copy in copies:
            copy.wait_recv()
        far = jnp.where(lower_p[None], gg_v[e, 3] * above, gg_v[e, 2] * below)
        parts = (gg_v[e, 0], gs_v[e], gg_v[e, 1], far)
        for block, part in enumerate(parts):
            part = part.reshape(32, 256)
            high = part.astype(BF16)
            low = (part - high.astype(F32)).astype(BF16)
            mm_v[pl.ds(32 * block, 32), :] = high
            mm_v[pl.ds(128 + 32 * block, 32), :] = high
            ml_v[pl.ds(32 * block, 32), :] = low

    def picked(tile, r):
        return jnp.where(row == r, tile, 0.0).astype(BF16)

    def mixer(r):
        p, q, f = r // 4, (r // 2) % 2, r % 2
        return (mixh_v if f else mixl_v)[p, q]

    loads[0].wait()
    loads[1].wait()
    partial_lat_start(0, x_v[...], None)
    pl.semaphore_wait(barrier, len(near))
    copies = partial_lat_send(0)

    loads[2].wait()
    loads[3].wait()
    ku_v[...] = kd_v[...].T
    xt_v[...] = x_v[...].T
    wt_v[...] = w_v[...].T
    loads[4].wait()
    loads[5].wait()
    loads[6].wait()

    copies = partial_lon(0, copies)
    coarse = partial_done(0, copies).astype(BF16).astype(F32)
    mixed = jnp.dot(picked(coarse, 0), mixer(0), preferred_element_type=F32)
    for r in range(1, 8):
        mixed = mixed + jnp.dot(picked(coarse, r), mixer(r), preferred_element_type=F32)
    copies = spread_lon(0, mixed)
    copies = spread_lat(0, copies)
    spread_done(0, copies)

    bacc_v[...] = jnp.zeros_like(bacc_v)
    chunk = 256

    def gate(i, carry):
        rows = pl.ds(pl.multiple_of(i * chunk, chunk), chunk)
        pre = jnp.dot(ku_v[rows, :], mm_v[...], preferred_element_type=F32)
        pre = pre + jnp.dot(ku_v[rows, :128], ml_v[...], preferred_element_type=F32)
        pre = pre + jnp.dot(x_v[rows, :], w_v[...], preferred_element_type=F32)
        pre = pre + bias_v[...]
        cdf = 0.5 * (1.0 + lax.erf(pre * (1.0 / math.sqrt(2.0))))
        pdf = jnp.exp(-0.5 * pre * pre) * (1.0 / math.sqrt(2.0 * math.pi))
        grad = cot_v[rows, :].astype(F32) * (cdf + pre * pdf)
        high = grad.astype(BF16)
        ghi_v[rows, :] = high
        glo_v[rows, :] = (grad - high.astype(F32)).astype(BF16)
        bacc_v[...] += jnp.sum(grad.reshape(chunk // 8, 8, 256), axis=0)
        return carry

    lax.fori_loop(0, 1024 // chunk, gate, 0)

    total = jnp.dot(xt_v[...], ghi_v[...], preferred_element_type=F32)
    for h in range(2):
        cs_v[h] = total[:, h * 128 : (h + 1) * 128].reshape(32, 8, 128)
    sem = iter(range(r_send.shape[0]))

    def send(src, dst, device):
        k = next(sem)
        return push(src, dst, r_send.at[k], r_recv.at[k], device)

    core_copy = send(cs_v.at[1 - core], cr_v, partner)
    bias_sum = jnp.sum(bacc_v[...], axis=0, keepdims=True)
    bs_v[0, 0:1] = bias_sum[:, :128]
    bs_v[0, 1:2] = bias_sum[:, 128:]
    bias_core = send(bs_v.at[0], bc_v, partner)

    partial_lat_start(1, ghi_v[...], glo_v[...])
    copies = partial_lat_send(1)

    z_order = sorted(range(nz), key=lambda k: -min(k, nz - k))
    x_order = sorted(range(1, nx), key=lambda k: -min(k, nx - k))
    y_order = sorted(range(1, ny), key=lambda k: -min(k, ny - k))
    cuts = sorted({0, 1, 3, 5, nz})
    groups = [(i, j) for i, j in zip(cuts, cuts[1:]) if j <= nz]
    if nz < 8:
        groups = [(i, i + 1) for i in range(nz)]

    core_copy.wait_recv()
    x_copies = []
    for start, stop in groups:
        waits = []
        for i in range(start, stop):
            part = pl.ds((x * nz + at_z(z_order[i])) * tz, tz)
            xr_v[x, i] = cs_v[core, part] + cr_v[part]
        for d, k in enumerate(x_order):
            for i in range(start, stop):
                part = pl.ds((at_x(k) * nz + at_z(z_order[i])) * tz, tz)
                xs_v[d, i] = cs_v[core, part] + cr_v[part]
            span = pl.ds(start, stop - start)
            waits.append(send(xs_v.at[d, span], xr_v.at[x, span], {"lon": at_x(k) * ny + y}))
        x_copies.append(waits)

    def bias_spread(i, order, slot, device):
        bs_v[i] = bias_part
        br_v[i, slot] = bias_part
        return [send(bs_v.at[i], br_v.at[i, slot], device(k)) for k in order]

    def bias_add(i, count, waits):
        for copy in waits:
            copy.wait_recv()
        whole = br_v[i, 0]
        for j in range(1, count):
            whole = whole + br_v[i, j]
        return whole

    bias_core.wait_recv()
    bias_part = bs_v[0] + bc_v[...]
    bias_waits = bias_spread(1, x_order, x, lambda k: {"lon": at_x(k) * ny + y})

    copies = partial_lon(1, copies)

    z_copies = []
    for (start, stop), waits in zip(groups, x_copies):
        for copy in waits:
            copy.wait_recv()
        for i in range(start, stop):
            k = z_order[i]
            part = xr_v[0, i]
            for j in range(1, nx):
                part = part + xr_v[j, i]
            if k == 0:
                zr_v[z] = part
            else:
                zs_v[i] = part
                z_copies.append(send(zs_v.at[i], zr_v.at[z], {"lat": at_z(k) * 2 + core}))
    bias_part = bias_add(1, nx, bias_waits)
    bias_waits = bias_spread(2, z_order[:-1], z, lambda k: {"lat": at_z(k) * 2 + core})

    back = partial_done(1, copies)
    back_rounded = back.astype(BF16).astype(F32)
    pull = None
    for r in range(8):
        term = lax.dot_general(picked(back_rounded, r), mixer(r), (((1,), (1,)), ((), ())),
                               preferred_element_type=F32)
        pull = term if pull is None else pull + term
    copies = spread_lon(1, pull)

    for copy in z_copies:
        copy.wait_recv()
    red = zr_v[0]
    for j in range(1, nz):
        red = red + zr_v[j]
    ys_v[...] = red
    yr_v[y] = red
    y_copies = [send(ys_v, yr_v.at[y], {"lon": x * ny + at_y(k)}) for k in y_order]
    bias_part = bias_add(2, nz, bias_waits)
    bias_waits = bias_spread(3, y_order, y, lambda k: {"lon": x * ny + at_y(k)})

    copies = spread_lat(1, copies)

    columns = coarse.T
    for r in range(8):
        p, q, f = r // 4, (r // 2) % 2, r % 2
        outer = (columns[:, r : r + 1] * back[r : r + 1, :]).astype(BF16)
        (mhg_v if f else mlg_v)[p, q] = outer

    for copy in y_copies:
        copy.wait_recv()
    red = yr_v[0]
    for j in range(1, ny):
        red = red + yr_v[j]
    af_v[core, x, z] = red * (1.0 / math.sqrt(ncells))

    def own(k):
        return af_v.at[core, x, lax.rem(z - k + nz, nz)]

    z_copies = {}
    for k in z_order[:-1]:
        z_copies[k] = send(own(0), own(0), {"lat": at_z(k) * 2 + core})
    x_copies = {k: [] for k in x_order}
    for k in x_order:
        x_copies[k].append(send(own(0), own(0), {"lon": at_x(k) * ny + y}))

    spread_done(1, copies)

    def back_out(i, carry):
        rows = pl.ds(pl.multiple_of(i * chunk, chunk), chunk)
        out = jnp.dot(ku_v[rows, :], mm_v[...], preferred_element_type=F32)
        out = out + jnp.dot(ku_v[rows, :128], ml_v[...], preferred_element_type=F32)
        out = out + jnp.dot(ghi_v[rows, :], wt_v[...], preferred_element_type=F32)
        fg_v[rows, :] = out.astype(BF16)
        return carry

    lax.fori_loop(0, 1024 // chunk, back_out, 0)

    for k in reversed(z_order[:-1]):
        z_copies[k].wait_recv()
        for j in x_order:
            x_copies[j].append(send(own(k), own(k), {"lon": at_x(j) * ny + y}))
    core_copies = [send(af_v.at[core, x], af_v.at[core, x], partner)]
    bg_v[...] = bias_add(3, ny, bias_waits) * (1.0 / math.sqrt(ncells))
    for k in reversed(x_order):
        for copy in x_copies[k]:
            copy.wait_recv()
        block = af_v.at[core, lax.rem(x - k + nx, nx)]
        core_copies.append(send(block, block, partner))
    for copy in core_copies:
        copy.wait_recv()
    for copy in sends:
        copy.wait_send()


def leave(fg_v, mlg_v, mhg_v, af_v, bias_v, fg_hbm, mlg_hbm, mhg_hbm, wg_hbm, bg_hbm,
          wg_v, bg_v, sem):
    copies = [
        pltpu.make_async_copy(fg_v, fg_hbm, sem.at[0]),
        pltpu.make_async_copy(mlg_v, mlg_hbm, sem.at[1]),
        pltpu.make_async_copy(mhg_v, mhg_hbm, sem.at[2]),
        pltpu.make_async_copy(wg_v, wg_hbm, sem.at[3]),
        pltpu.make_async_copy(bg_v, bg_hbm, sem.at[4]),
    ]
    for copy in copies[:3]:
        copy.start()
    for h in range(2):
        wg_v[:, h * 128 : (h + 1) * 128] = af_v[h].reshape(256, 128)
        bg_v[:, h * 128 : (h + 1) * 128] = bias_v[h : h + 1]
    for copy in copies[3:]:
        copy.start()
    for copy in copies:
        copy.wait()


def shards(fields, cotangent, mix_low, mix_high, point_weight, point_bias):
    nlat, nlon = lax.axis_size("lat"), lax.axis_size("lon")
    rows, cols, channels = fields.shape
    cells = rows * cols
    tables = jnp.asarray(band_tables(rows * nlat, cols * nlon, rows, cols))
    nz, ny = nlat // 2, min(ROW, nlon // 2)
    nx = nlon // ny
    tx = 32 // nx
    tz = tx // nz
    groups = 4 if nz == 8 else nz
    messages = 2 + groups * (nx - 1) + (nx - 1) + 2 * (nz - 1) + 2 * (ny - 1)
    messages += (nz - 1) + nz * (nx - 1) + nx
    vmem = pltpu.VMEM
    scratch = [
        vmem((cells, channels), BF16), vmem((cells, channels), BF16),
        vmem(mix_low.shape, BF16), vmem(mix_high.shape, BF16),
        vmem((channels, channels), BF16), vmem((1, channels), F32), vmem((256, cells), BF16),
        vmem((cells, 256), BF16), vmem((channels, cells), BF16), vmem((channels, channels), BF16),
        vmem((cells, channels), BF16), vmem((cells, channels), BF16),
        vmem((256, channels), BF16), vmem((128, channels), BF16), vmem((8, channels), F32),
        vmem((2, 4, 4, 8, channels), F32), vmem((2, 4, 4, 8, channels), F32),
        vmem((2, 4, 8, channels), F32), vmem((2, 4, 8, channels), F32),
        vmem((2, 8, channels), F32), vmem((2, 4, 8, channels), F32),
        vmem((2, 4, 8, channels), F32), vmem((2, 4, 4, 8, channels), F32),
        vmem((2, 32, 8, 128), F32), vmem((32, 8, 128), F32),
        vmem((nx - 1, nz, tz, 8, 128), F32), vmem((nx, nz, tz, 8, 128), F32),
        vmem((nz, tz, 8, 128), F32), vmem((nz, tz, 8, 128), F32),
        vmem((tz, 8, 128), F32), vmem((ny, tz, 8, 128), F32),
        vmem((4, 2, 128), F32), vmem((2, 128), F32), vmem((4, max(nx, ny, nz), 2, 128), F32),
        pltpu.SemaphoreType.DMA((7,)),
        pltpu.SemaphoreType.DMA((2, 4, 4)), pltpu.SemaphoreType.DMA((2, 4, 4)),
        pltpu.SemaphoreType.DMA((messages,)), pltpu.SemaphoreType.DMA((messages,)),
    ]
    outs = pl.pallas_call(
        functools.partial(kernel, (nlat, nlon, cells * nlat * nlon)),
        out_shape=(
            jax.ShapeDtypeStruct((cells, channels), BF16),
            jax.ShapeDtypeStruct(mix_low.shape, BF16),
            jax.ShapeDtypeStruct(mix_high.shape, BF16),
            jax.ShapeDtypeStruct((2, nx, nz, tz, 8, 128), F32),
            jax.ShapeDtypeStruct((2, 128), F32),
        ),
        in_specs=[pl.BlockSpec(memory_space=pltpu.HBM)] * 7,
        out_specs=[pl.BlockSpec(memory_space=vmem)] * 5,
        scratch_shapes=scratch,
        compiler_params=pltpu.CompilerParams(
            collective_id=0, has_side_effects=True, vmem_limit_bytes=32 * 1024 * 1024
        ),
        name="wavelet_block",
    )(*[
        pltpu.with_memory_space_constraint(array, pltpu.HBM)
        for array in (
            fields.reshape(cells, channels), cotangent.reshape(cells, channels), mix_low, mix_high,
            point_weight, point_bias.reshape(1, channels), tables,
        )
    ])
    outs = pl.pallas_call(
        leave,
        out_shape=(
            jax.ShapeDtypeStruct((cells, channels), BF16),
            jax.ShapeDtypeStruct(mix_low.shape, BF16),
            jax.ShapeDtypeStruct(mix_high.shape, BF16),
            jax.ShapeDtypeStruct((channels, channels), F32),
            jax.ShapeDtypeStruct((1, channels), F32),
        ),
        in_specs=[pl.BlockSpec(memory_space=vmem)] * 5,
        out_specs=[pl.BlockSpec(memory_space=pltpu.HBM)] * 5,
        scratch_shapes=[
            vmem((channels, channels), F32), vmem((1, channels), F32),
            pltpu.SemaphoreType.DMA((5,)),
        ],
        compiler_params=pltpu.CompilerParams(vmem_limit_bytes=16 * 1024 * 1024),
        name="leave",
    )(outs[0], outs[1], outs[2], outs[3].reshape(2, 32, 8, 128), outs[4])
    return (
        outs[0].reshape(fields.shape), outs[1], outs[2], outs[3], outs[4].reshape(channels),
    )


def solution(mesh):
    placed = (
        P("lat", "lon", None),
        P("lat", "lon", None),
        P("lat", "lon", None, None),
        P("lat", "lon", None, None),
        P(),
        P(),
    )
    return jax.shard_map(
        shards,
        mesh=mesh,
        in_specs=placed,
        out_specs=(
            P("lat", "lon", None),
            P("lat", "lon", None, None),
            P("lat", "lon", None, None),
            P(),
            P(),
        ),
        check_vma=False,
    )
```

```python
import functools
import math

import jax
import jax.numpy as jnp
import numpy as np
from jax import lax
from jax.experimental import pallas as pl
from jax.experimental.pallas import tpu as pltpu
from jax.sharding import PartitionSpec as P

MESH = pl.DeviceIdType.MESH
F32 = jnp.float32
BF16 = jnp.bfloat16
ROW = 8

low_taps = (
    -0.010597401784997278,
    0.032883011666982945,
    0.030841381835986965,
    -0.18703481171888114,
    -0.02798376941698385,
    0.6308807679295904,
    0.7148465705525415,
    0.23037781330885523,
)
high_taps = (
    -0.23037781330885523,
    0.7148465705525415,
    -0.6308807679295904,
    -0.02798376941698385,
    0.18703481171888114,
    0.030841381835986965,
    -0.032883011666982945,
    -0.010597401784997278,
)


def level_matrix(count, taps, closed):
    matrix = np.zeros((count // 2, count))
    for k in range(count // 2):
        for j in range(8):
            n = 2 * k + j - 3
            if closed:
                matrix[k, n % count] += taps[j]
            elif 0 <= n < count:
                matrix[k, n] += taps[j]
    return matrix


def analysis_matrix(count, last_taps, closed):
    product = level_matrix(count, low_taps, closed)
    for level in (1, 2):
        product = level_matrix(count >> level, low_taps, closed) @ product
    return level_matrix(count >> 3, last_taps, closed) @ product


def coarse_offset(block, half):
    if block < 3:
        return 2 * (block - 1) + half
    return -3 if half == 1 else 4


def band_tables(nlat, nlon, band, sector):
    lat = analysis_matrix(nlat, low_taps, False)
    lons = [analysis_matrix(nlon, taps, True) for taps in (low_taps, high_taps)]
    bands = nlat // band
    tables = []
    for d in (0, bands // 2, bands - 1):
        rows = np.zeros((4, 2, band))
        for block in range(4):
            for p in range(2):
                k = 2 * d + coarse_offset(block, p)
                if 0 <= k < lat.shape[0]:
                    rows[block, p] = lat[k, d * band : (d + 1) * band]
        cols = np.zeros((4, 2, 2, sector))
        for block in range(4):
            for q in range(2):
                k = (2 + coarse_offset(block, q)) % lons[0].shape[0]
                for f in range(2):
                    cols[block, q, f] = lons[f][k, sector : 2 * sector]
        table = np.einsum("apn,bqfm->abpqfnm", rows, cols)
        table[:3, 3] = table[:3, 3].transpose(0, 2, 1, 3, 4, 5)
        tables.append(table.reshape(128, band * sector))
    full = np.stack(tables).astype(np.float32)
    high = full.astype(jnp.bfloat16)
    low = (full - high.astype(np.float32)).astype(jnp.bfloat16)
    return np.concatenate([high, low], axis=1)


def offsets():
    steps = [(i, j) for i in range(-2, 3) for j in range(-2, 3) if (i, j) != (0, 0)]
    return sorted(steps, key=lambda s: -(abs(s[1]) + abs(s[0]) / 2))


def place(i, j):
    a = 3 if abs(i) == 2 else i + 1
    b = 3 if abs(j) == 2 else j + 1
    start, size = 0, 8
    if a == 3 and b == 3:
        start, size = (4 if i < 0 else 0) + (2 if j < 0 else 0), 2
    elif a == 3:
        start, size = (4 if i < 0 else 0), 4
    elif b == 3:
        start, size = (4 if j < 0 else 0), 4
    return a, b, pl.ds(start, size)


def kernel(
    dims, x_hbm, cot_hbm, mixl_hbm, mixh_hbm, w_hbm, bias_hbm, k_hbm,
    fg_v, mlg_v, mhg_v, af_v, bg_v,
    x_v, cot_v, mixl_v, mixh_v, w_v, bias_v, kd_v,
    ku_v, xt_v, wt_v, ghi_v, glo_v, mm_v, ml_v, bacc_v,
    as_v, ar_v, gm_v, gg_v,
    cs_v, cr_v, xs_v, xr_v, zs_v, zr_v, ys_v, yr_v,
    bs_v, bc_v, br_v,
    in_sem, h_send, h_recv, r_send, r_recv,
):
    nlat, nlon, ncells = dims
    nz, ny = nlat // 2, min(ROW, nlon // 2)
    nx = nlon // ny
    tx = 32 // nx
    tz = tx // nz
    lat, lon = lax.axis_index("lat"), lax.axis_index("lon")
    core, z = lax.rem(lat, 2), lat // 2
    y, x = lax.rem(lon, ny), lon // ny

    def at(i, j):
        return (lax.rem(lat + i + nlat, nlat), lax.rem(lon + j + nlon, nlon))

    other = lat + 1 - 2 * core
    partner = {"lat": other}

    def at_z(k):
        return lax.rem(z + k, nz)

    def at_x(k):
        return lax.rem(x + k, nx)

    def at_y(k):
        return lax.rem(y + k, ny)

    variant = (lat + nlat - 2) // (nlat - 1) + lat // (nlat - 1)
    loads = [
        (x_hbm, x_v), (k_hbm.at[variant], kd_v), (w_hbm, w_v), (bias_hbm, bias_v),
        (mixl_hbm, mixl_v), (mixh_hbm, mixh_v), (cot_hbm, cot_v),
    ]
    loads = [pltpu.make_async_copy(s, d, in_sem.at[i]) for i, (s, d) in enumerate(loads)]
    for copy in loads[:2]:
        copy.start()

    barrier = pltpu.get_barrier_semaphore()
    near = [at(i, j) for i, j in offsets()]
    near += [{"lat": at_z(k) * 2 + core} for k in range(1, nz)]
    near += [(side, at_x(k) * ny + y) for k in range(1, nx) for side in (lat, other)]
    near += [{"lon": x * ny + at_y(k)} for k in range(1, ny)]
    for device in near:
        pl.semaphore_signal(barrier, inc=1, device_id=device, device_id_type=MESH)

    sends = []

    def push(src, dst, send_sem, recv_sem, device):
        copy = pltpu.make_async_remote_copy(
            src_ref=src, dst_ref=dst, send_sem=send_sem, recv_sem=recv_sem,
            device_id=device, device_id_type=MESH,
        )
        copy.start()
        sends.append(copy)
        return copy

    row = lax.broadcasted_iota(jnp.int32, (8, 256), 0)
    below = jnp.where(lat >= 2, 1.0, 0.0)
    above = jnp.where(lat + 2 < nlat, 1.0, 0.0)
    edge_sum = jnp.where(row < 4, below, above)
    edge_take = jnp.where(row < 4, above, below)

    def swapped(tile):
        up, down = pltpu.roll(tile, 6, 0), pltpu.roll(tile, 2, 0)
        tile = jnp.where(row // 2 == 1, up, tile)
        return jnp.where(row // 2 == 2, down, tile)

    def partial_start(e, hi, lo):
        whole = jnp.dot(kd_v[...], hi, preferred_element_type=F32)
        part = whole[:128] + whole[128:]
        if lo is not None:
            part = part + jnp.dot(kd_v[:128], lo, preferred_element_type=F32)
        as_v[e] = part.reshape(4, 4, 8, 256)

    def partial_send(e):
        copies = []
        for n, (i, j) in enumerate(offsets()):
            spot = (e,) + place(i, j)
            copies.append(push(as_v.at[spot], ar_v.at[spot], h_send.at[2 * e, n],
                               h_recv.at[2 * e, n], at(i, j)))
        return copies

    def partial_done(e, copies):
        for copy in copies:
            copy.wait_recv()
        total = as_v[e, 1, 1]
        for a in range(3):
            for b in range(3):
                if (a, b) != (1, 1):
                    total = total + ar_v[e, a, b]
        far = (ar_v[e, 3, 0] + ar_v[e, 3, 1]) + (ar_v[e, 3, 2] + ar_v[e, 3, 3])
        side = ar_v[e, 0, 3] + ar_v[e, 1, 3] + ar_v[e, 2, 3]
        return total + far * edge_sum + swapped(side)

    def spread(e, tile):
        gm_v[e, 0] = tile
        gm_v[e, 1] = swapped(tile)
        gg_v[e, 1, 1] = tile
        copies = []
        for n, (i, j) in enumerate(offsets()):
            a, b, rows = place(-i, -j)
            form = 1 if b == 3 and a < 3 else 0
            copies.append(push(gm_v.at[e, form, rows], gg_v.at[e, a, b, rows],
                               h_send.at[2 * e + 1, n], h_recv.at[2 * e + 1, n], at(i, j)))
        return copies

    def spread_done(e, copies):
        for copy in copies:
            copy.wait_recv()
        for block in range(4):
            part = gg_v[e, block]
            if block == 3:
                part = part * edge_take[None]
            part = part.reshape(32, 256)
            high = part.astype(BF16)
            low = (part - high.astype(F32)).astype(BF16)
            mm_v[pl.ds(32 * block, 32), :] = high
            mm_v[pl.ds(128 + 32 * block, 32), :] = high
            ml_v[pl.ds(32 * block, 32), :] = low

    def picked(tile, r):
        return jnp.where(row == r, tile, 0.0).astype(BF16)

    def mixer(r):
        p, q, f = r // 4, (r // 2) % 2, r % 2
        return (mixh_v if f else mixl_v)[p, q]

    loads[0].wait()
    loads[1].wait()
    for copy in loads[2:]:
        copy.start()
    partial_start(0, x_v[...], None)
    pl.semaphore_wait(barrier, len(near))
    copies = partial_send(0)

    loads[2].wait()
    loads[3].wait()
    ku_v[...] = kd_v[...].T
    xt_v[...] = x_v[...].T
    wt_v[...] = w_v[...].T
    loads[4].wait()
    loads[5].wait()
    loads[6].wait()

    coarse = partial_done(0, copies).astype(BF16).astype(F32)
    mixed = jnp.dot(picked(coarse, 0), mixer(0), preferred_element_type=F32)
    for r in range(1, 8):
        mixed = mixed + jnp.dot(picked(coarse, r), mixer(r), preferred_element_type=F32)
    copies = spread(0, mixed)
    spread_done(0, copies)

    bacc_v[...] = jnp.zeros_like(bacc_v)
    chunk = 256

    def gate(i, carry):
        rows = pl.ds(pl.multiple_of(i * chunk, chunk), chunk)
        pre = jnp.dot(ku_v[rows, :], mm_v[...], preferred_element_type=F32)
        pre = pre + jnp.dot(ku_v[rows, :128], ml_v[...], preferred_element_type=F32)
        pre = pre + jnp.dot(x_v[rows, :], w_v[...], preferred_element_type=F32)
        pre = pre + bias_v[...]
        cdf = 0.5 * (1.0 + lax.erf(pre * (1.0 / math.sqrt(2.0))))
        pdf = jnp.exp(-0.5 * pre * pre) * (1.0 / math.sqrt(2.0 * math.pi))
        grad = cot_v[rows, :].astype(F32) * (cdf + pre * pdf)
        high = grad.astype(BF16)
        ghi_v[rows, :] = high
        glo_v[rows, :] = (grad - high.astype(F32)).astype(BF16)
        bacc_v[...] += jnp.sum(grad.reshape(chunk // 8, 8, 256), axis=0)
        return carry

    lax.fori_loop(0, 1024 // chunk, gate, 0)

    total = jnp.dot(xt_v[...], ghi_v[...], preferred_element_type=F32)
    for h in range(2):
        cs_v[h] = total[:, h * 128 : (h + 1) * 128].reshape(nx, nz, tz, 8, 128)
    sem = iter(range(r_send.shape[0]))

    def send(src, dst, device):
        k = next(sem)
        return push(src, dst, r_send.at[k], r_recv.at[k], device)

    z_order = sorted(range(nz), key=lambda k: -min(k, nz - k))
    x_order = sorted(range(1, nx), key=lambda k: -min(k, nx - k))
    y_order = sorted(range(1, ny), key=lambda k: -min(k, ny - k))
    cuts = sorted({0, 1, 3, 5, nz}) if nz == 8 else range(nz + 1)
    groups = list(zip(cuts, cuts[1:]))

    core_copies = [
        send(cs_v.at[1 - core, :, at_z(k)], cr_v.at[:, at_z(k)], partner) for k in z_order
    ]
    bias_sum = jnp.sum(bacc_v[...], axis=0, keepdims=True)
    bs_v[0, 0:1] = bias_sum[:, :128]
    bs_v[0, 1:2] = bias_sum[:, 128:]
    bias_core = send(bs_v.at[0], bc_v, partner)

    partial_start(1, ghi_v[...], glo_v[...])
    copies = partial_send(1)

    x_copies = []
    for start, stop in groups:
        waits = []
        for i in range(start, stop):
            core_copies[i].wait_recv()
            zi = at_z(z_order[i])
            xr_v[x, i] = cs_v[core, x, zi] + cr_v[x, zi]
        for d, k in enumerate(x_order):
            for i in range(start, stop):
                xi, zi = at_x(k), at_z(z_order[i])
                xs_v[d, i] = cs_v[core, xi, zi] + cr_v[xi, zi]
            span = pl.ds(start, stop - start)
            waits.append(send(xs_v.at[d, span], xr_v.at[x, span], {"lon": at_x(k) * ny + y}))
        x_copies.append(waits)

    def bias_spread(i, order, slot, device):
        bs_v[i] = bias_part
        br_v[i, slot] = bias_part
        return [send(bs_v.at[i], br_v.at[i, slot], device(k)) for k in order]

    def bias_add(i, count, waits):
        for copy in waits:
            copy.wait_recv()
        whole = br_v[i, 0]
        for j in range(1, count):
            whole = whole + br_v[i, j]
        return whole

    bias_core.wait_recv()
    bias_part = bs_v[0] + bc_v[...]
    bias_waits = bias_spread(1, x_order, x, lambda k: {"lon": at_x(k) * ny + y})

    z_copies = []
    for (start, stop), waits in zip(groups, x_copies):
        for copy in waits:
            copy.wait_recv()
        for i in range(start, stop):
            k = z_order[i]
            part = xr_v[0, i]
            for j in range(1, nx):
                part = part + xr_v[j, i]
            if k == 0:
                zr_v[z] = part
            else:
                zs_v[i] = part
                z_copies.append(send(zs_v.at[i], zr_v.at[z], {"lat": at_z(k) * 2 + core}))
    bias_part = bias_add(1, nx, bias_waits)
    bias_waits = bias_spread(2, z_order[:-1], z, lambda k: {"lat": at_z(k) * 2 + core})

    back = partial_done(1, copies)
    back_rounded = back.astype(BF16).astype(F32)
    pull = None
    for r in range(8):
        term = lax.dot_general(picked(back_rounded, r), mixer(r), (((1,), (1,)), ((), ())),
                               preferred_element_type=F32)
        pull = term if pull is None else pull + term
    copies = spread(1, pull)

    for copy in z_copies:
        copy.wait_recv()
    red = zr_v[0]
    for j in range(1, nz):
        red = red + zr_v[j]
    ys_v[...] = red
    yr_v[y] = red
    y_copies = [send(ys_v, yr_v.at[y], {"lon": x * ny + at_y(k)}) for k in y_order]
    bias_part = bias_add(2, nz, bias_waits)
    bias_waits = bias_spread(3, y_order, y, lambda k: {"lon": x * ny + at_y(k)})

    columns = coarse.T
    for r in range(8):
        p, q, f = r // 4, (r // 2) % 2, r % 2
        outer = (columns[:, r : r + 1] * back[r : r + 1, :]).astype(BF16)
        (mhg_v if f else mlg_v)[p, q] = outer

    for copy in y_copies:
        copy.wait_recv()
    red = yr_v[0]
    for j in range(1, ny):
        red = red + yr_v[j]
    af_v[core, x, z] = red * (1.0 / math.sqrt(ncells))

    last = z_order[0]
    sooner = list(reversed(z_order[1:]))

    def own(k):
        return af_v.at[core, x, lax.rem(z - k + nz, nz)]

    z_copies = {}
    for k in z_order[:-1]:
        z_copies[k] = send(own(0), own(0), {"lat": at_z(k) * 2 + core})
    x_copies = {}
    x_copies[0] = [send(own(0), own(0), {"lon": at_x(j) * ny + y}) for j in x_order]

    spread_done(1, copies)

    def back_out(i, carry):
        rows = pl.ds(pl.multiple_of(i * chunk, chunk), chunk)
        out = jnp.dot(ku_v[rows, :], mm_v[...], preferred_element_type=F32)
        out = out + jnp.dot(ku_v[rows, :128], ml_v[...], preferred_element_type=F32)
        out = out + jnp.dot(ghi_v[rows, :], wt_v[...], preferred_element_type=F32)
        fg_v[rows, :] = out.astype(BF16)
        return carry

    lax.fori_loop(0, 1024 // chunk, back_out, 0)

    for k in sooner[1:]:
        z_copies[k].wait_recv()
        x_copies[k] = [send(own(k), own(k), {"lon": at_x(j) * ny + y}) for j in x_order]
    z_copies[last].wait_recv()
    arrivals = [
        send(own(last), own(last), (side, at_x(j) * ny + y))
        for j in x_order for side in (lat, other)
    ]
    arrivals.append(send(own(last), own(last), partner))
    bg_v[...] = bias_add(3, ny, bias_waits) * (1.0 / math.sqrt(ncells))
    for k in sooner:
        for copy in x_copies[k]:
            copy.wait_recv()
        column = af_v.at[core, :, lax.rem(z - k + nz, nz)]
        arrivals.append(send(column, column, partner))
    for copy in arrivals:
        copy.wait_recv()
    for copy in sends:
        copy.wait_send()


def leave(fg_v, mlg_v, mhg_v, af_v, bias_v, fg_hbm, mlg_hbm, mhg_hbm, wg_hbm, bg_hbm,
          wg_v, bg_v, sem):
    copies = [
        pltpu.make_async_copy(fg_v, fg_hbm, sem.at[0]),
        pltpu.make_async_copy(mlg_v, mlg_hbm, sem.at[1]),
        pltpu.make_async_copy(mhg_v, mhg_hbm, sem.at[2]),
        pltpu.make_async_copy(wg_v, wg_hbm, sem.at[3]),
        pltpu.make_async_copy(bg_v, bg_hbm, sem.at[4]),
    ]
    for copy in copies[:3]:
        copy.start()
    for h in range(2):
        wg_v[:, h * 128 : (h + 1) * 128] = af_v[h].reshape(256, 128)
        bg_v[:, h * 128 : (h + 1) * 128] = bias_v[h : h + 1]
    for copy in copies[3:]:
        copy.start()
    for copy in copies:
        copy.wait()


def shards(fields, cotangent, mix_low, mix_high, point_weight, point_bias):
    nlat, nlon = lax.axis_size("lat"), lax.axis_size("lon")
    rows, cols, channels = fields.shape
    cells = rows * cols
    tables = jnp.asarray(band_tables(rows * nlat, cols * nlon, rows, cols))
    nz, ny = nlat // 2, min(ROW, nlon // 2)
    nx = nlon // ny
    tx = 32 // nx
    tz = tx // nz
    messages = 2 * nz + nz * (nx - 1) + (nx - 1) + 3 * (nz - 1) + 2 * (ny - 1)
    messages += (nz + 1) * (nx - 1) + 1
    vmem = pltpu.VMEM
    scratch = [
        vmem((cells, channels), BF16), vmem((cells, channels), BF16),
        vmem(mix_low.shape, BF16), vmem(mix_high.shape, BF16),
        vmem((channels, channels), BF16), vmem((1, channels), F32), vmem((256, cells), BF16),
        vmem((cells, 256), BF16), vmem((channels, cells), BF16), vmem((channels, channels), BF16),
        vmem((cells, channels), BF16), vmem((cells, channels), BF16),
        vmem((256, channels), BF16), vmem((128, channels), BF16), vmem((8, channels), F32),
        vmem((2, 4, 4, 8, channels), F32), vmem((2, 4, 4, 8, channels), F32),
        vmem((2, 2, 8, channels), F32), vmem((2, 4, 4, 8, channels), F32),
        vmem((2, nx, nz, tz, 8, 128), F32), vmem((nx, nz, tz, 8, 128), F32),
        vmem((nx - 1, nz, tz, 8, 128), F32), vmem((nx, nz, tz, 8, 128), F32),
        vmem((nz, tz, 8, 128), F32), vmem((nz, tz, 8, 128), F32),
        vmem((tz, 8, 128), F32), vmem((ny, tz, 8, 128), F32),
        vmem((4, 2, 128), F32), vmem((2, 128), F32), vmem((4, max(nx, ny, nz), 2, 128), F32),
        pltpu.SemaphoreType.DMA((7,)),
        pltpu.SemaphoreType.DMA((4, 24)), pltpu.SemaphoreType.DMA((4, 24)),
        pltpu.SemaphoreType.DMA((messages,)), pltpu.SemaphoreType.DMA((messages,)),
    ]
    outs = pl.pallas_call(
        functools.partial(kernel, (nlat, nlon, cells * nlat * nlon)),
        out_shape=(
            jax.ShapeDtypeStruct((cells, channels), BF16),
            jax.ShapeDtypeStruct(mix_low.shape, BF16),
            jax.ShapeDtypeStruct(mix_high.shape, BF16),
            jax.ShapeDtypeStruct((2, nx, nz, tz, 8, 128), F32),
            jax.ShapeDtypeStruct((2, 128), F32),
        ),
        in_specs=[pl.BlockSpec(memory_space=pltpu.HBM)] * 7,
        out_specs=[pl.BlockSpec(memory_space=vmem)] * 5,
        scratch_shapes=scratch,
        compiler_params=pltpu.CompilerParams(
            collective_id=0, has_side_effects=True, vmem_limit_bytes=32 * 1024 * 1024
        ),
        name="wavelet_block",
    )(*[
        pltpu.with_memory_space_constraint(array, pltpu.HBM)
        for array in (
            fields.reshape(cells, channels), cotangent.reshape(cells, channels), mix_low, mix_high,
            point_weight, point_bias.reshape(1, channels), tables,
        )
    ])
    outs = pl.pallas_call(
        leave,
        out_shape=(
            jax.ShapeDtypeStruct((cells, channels), BF16),
            jax.ShapeDtypeStruct(mix_low.shape, BF16),
            jax.ShapeDtypeStruct(mix_high.shape, BF16),
            jax.ShapeDtypeStruct((channels, channels), F32),
            jax.ShapeDtypeStruct((1, channels), F32),
        ),
        in_specs=[pl.BlockSpec(memory_space=vmem)] * 5,
        out_specs=[pl.BlockSpec(memory_space=pltpu.HBM)] * 5,
        scratch_shapes=[
            vmem((channels, channels), F32), vmem((1, channels), F32),
            pltpu.SemaphoreType.DMA((5,)),
        ],
        compiler_params=pltpu.CompilerParams(vmem_limit_bytes=16 * 1024 * 1024),
        name="leave",
    )(outs[0], outs[1], outs[2], outs[3].reshape(2, 32, 8, 128), outs[4])
    return (
        outs[0].reshape(fields.shape), outs[1], outs[2], outs[3], outs[4].reshape(channels),
    )


def solution(mesh):
    placed = (
        P("lat", "lon", None),
        P("lat", "lon", None),
        P("lat", "lon", None, None),
        P("lat", "lon", None, None),
        P(),
        P(),
    )
    return jax.shard_map(
        shards,
        mesh=mesh,
        in_specs=placed,
        out_specs=(
            P("lat", "lon", None),
            P("lat", "lon", None, None),
            P("lat", "lon", None, None),
            P(),
            P(),
        ),
        check_vma=False,
    )
```

```python
import functools
import math

import jax
import jax.numpy as jnp
import numpy as np
from jax import lax
from jax.experimental import pallas as pl
from jax.experimental.pallas import tpu as pltpu
from jax.sharding import PartitionSpec as P

MESH = pl.DeviceIdType.MESH
F32 = jnp.float32
BF16 = jnp.bfloat16
ROW = 8

low_taps = (
    -0.010597401784997278,
    0.032883011666982945,
    0.030841381835986965,
    -0.18703481171888114,
    -0.02798376941698385,
    0.6308807679295904,
    0.7148465705525415,
    0.23037781330885523,
)
high_taps = (
    -0.23037781330885523,
    0.7148465705525415,
    -0.6308807679295904,
    -0.02798376941698385,
    0.18703481171888114,
    0.030841381835986965,
    -0.032883011666982945,
    -0.010597401784997278,
)


def level_matrix(count, taps, closed):
    matrix = np.zeros((count // 2, count))
    for k in range(count // 2):
        for j in range(8):
            n = 2 * k + j - 3
            if closed:
                matrix[k, n % count] += taps[j]
            elif 0 <= n < count:
                matrix[k, n] += taps[j]
    return matrix


def analysis_matrix(count, last_taps, closed):
    product = level_matrix(count, low_taps, closed)
    for level in (1, 2):
        product = level_matrix(count >> level, low_taps, closed) @ product
    return level_matrix(count >> 3, last_taps, closed) @ product


def coarse_offset(block, half):
    if block < 3:
        return 2 * (block - 1) + half
    return -3 if half == 1 else 4


def band_tables(nlat, nlon, band, sector):
    lat = analysis_matrix(nlat, low_taps, False)
    lons = [analysis_matrix(nlon, taps, True) for taps in (low_taps, high_taps)]
    bands = nlat // band
    tables = []
    for d in (0, bands // 2, bands - 1):
        rows = np.zeros((4, 2, band))
        for block in range(4):
            for p in range(2):
                k = 2 * d + coarse_offset(block, p)
                if 0 <= k < lat.shape[0]:
                    rows[block, p] = lat[k, d * band : (d + 1) * band]
        cols = np.zeros((4, 2, 2, sector))
        for block in range(4):
            for q in range(2):
                k = (2 + coarse_offset(block, q)) % lons[0].shape[0]
                for f in range(2):
                    cols[block, q, f] = lons[f][k, sector : 2 * sector]
        table = np.einsum("apn,bqfm->abpqfnm", rows, cols)
        table[:3, 3] = table[:3, 3].transpose(0, 2, 1, 3, 4, 5)
        tables.append(table.reshape(128, band * sector))
    full = np.stack(tables).astype(np.float32)
    high = full.astype(jnp.bfloat16)
    low = (full - high.astype(np.float32)).astype(jnp.bfloat16)
    return np.concatenate([high, low], axis=1)


def offsets():
    steps = [(i, j) for i in range(-2, 3) for j in range(-2, 3) if (i, j) != (0, 0)]
    return sorted(steps, key=lambda s: -(abs(s[1]) + abs(s[0]) / 2))


def place(i, j):
    a = 3 if abs(i) == 2 else i + 1
    b = 3 if abs(j) == 2 else j + 1
    start, size = 0, 8
    if a == 3 and b == 3:
        start, size = (4 if i < 0 else 0) + (2 if j < 0 else 0), 2
    elif a == 3:
        start, size = (4 if i < 0 else 0), 4
    elif b == 3:
        start, size = (4 if j < 0 else 0), 4
    return a, b, pl.ds(start, size)


def kernel(
    dims, x_hbm, cot_hbm, mixl_hbm, mixh_hbm, w_hbm, bias_hbm, k_hbm,
    fg_v, mlg_v, mhg_v, af_v, bg_v,
    x_v, cot_v, mixl_v, mixh_v, w_v, bias_v, kd_v,
    ku_v, xt_v, wt_v, ghi_v, glo_v, mm_v, ml_v, bacc_v,
    as_v, ar_v, gm_v, gg_v,
    cs_v, cr_v, xs_v, rr_v, ys_v, yr_v,
    bs_v, bc_v, br_v,
    in_sem, h_send, h_recv, r_send, r_recv, hello,
):
    nlat, nlon, ncells = dims
    nz, ny = nlat // 2, min(ROW, nlon // 2)
    nx = nlon // ny
    tx = 32 // nx
    tz = tx // nz
    lat, lon = lax.axis_index("lat"), lax.axis_index("lon")
    core, z = lax.rem(lat, 2), lat // 2
    y, x = lax.rem(lon, ny), lon // ny

    def at(i, j):
        return (lax.rem(lat + i + nlat, nlat), lax.rem(lon + j + nlon, nlon))

    other = lat + 1 - 2 * core
    partner = {"lat": other}

    def at_z(k):
        return lax.rem(z + k, nz)

    def at_x(k):
        return lax.rem(x + k, nx)

    def at_y(k):
        return lax.rem(y + k, ny)

    variant = (lat + nlat - 2) // (nlat - 1) + lat // (nlat - 1)
    loads = [
        (x_hbm, x_v), (k_hbm.at[variant], kd_v), (w_hbm, w_v), (bias_hbm, bias_v),
        (mixl_hbm, mixl_v), (mixh_hbm, mixh_v), (cot_hbm, cot_v),
    ]
    loads = [pltpu.make_async_copy(s, d, in_sem.at[i]) for i, (s, d) in enumerate(loads)]
    loads[0].start()

    barrier = pltpu.get_barrier_semaphore()
    near = [at(i, j) for i, j in offsets()]
    near += [{"lat": at_z(k) * 2 + core} for k in range(1, nz)]
    near += [(side, at_x(k) * ny + y) for k in range(1, nx) for side in (lat, other)]
    near += [{"lon": x * ny + at_y(k)} for k in range(1, ny)]
    for device in near:
        pl.semaphore_signal(barrier, inc=1, device_id=device, device_id_type=MESH)
    loads[1].start()

    sends = []

    def push(src, dst, send_sem, recv_sem, device):
        copy = pltpu.make_async_remote_copy(
            src_ref=src, dst_ref=dst, send_sem=send_sem, recv_sem=recv_sem,
            device_id=device, device_id_type=MESH,
        )
        copy.start()
        sends.append(copy)
        return copy

    row = lax.broadcasted_iota(jnp.int32, (8, 256), 0)
    below = jnp.where(lat >= 2, 1.0, 0.0)
    above = jnp.where(lat + 2 < nlat, 1.0, 0.0)
    edge_sum = jnp.where(row < 4, below, above)
    edge_take = jnp.where(row < 4, above, below)

    def swapped(tile):
        up, down = pltpu.roll(tile, 6, 0), pltpu.roll(tile, 2, 0)
        tile = jnp.where(row // 2 == 1, up, tile)
        return jnp.where(row // 2 == 2, down, tile)

    def partial_start(e, hi, lo):
        whole = jnp.dot(kd_v[...], hi, preferred_element_type=F32)
        part = whole[:128] + whole[128:]
        if lo is not None:
            part = part + jnp.dot(kd_v[:128], lo, preferred_element_type=F32)
        as_v[e] = part.reshape(4, 4, 8, 256)

    def partial_send(e):
        copies = []
        for n, (i, j) in enumerate(offsets()):
            spot = (e,) + place(i, j)
            copies.append(push(as_v.at[spot], ar_v.at[spot], h_send.at[2 * e, n],
                               h_recv.at[2 * e, n], at(i, j)))
        return copies

    def partial_done(e, copies):
        for copy in copies:
            copy.wait_recv()
        total = as_v[e, 1, 1]
        for a in range(3):
            for b in range(3):
                if (a, b) != (1, 1):
                    total = total + ar_v[e, a, b]
        far = (ar_v[e, 3, 0] + ar_v[e, 3, 1]) + (ar_v[e, 3, 2] + ar_v[e, 3, 3])
        side = ar_v[e, 0, 3] + ar_v[e, 1, 3] + ar_v[e, 2, 3]
        return total + far * edge_sum + swapped(side)

    def spread(e, tile):
        gm_v[e, 0] = tile
        gm_v[e, 1] = swapped(tile)
        gg_v[e, 1, 1] = tile
        copies = []
        for n, (i, j) in enumerate(offsets()):
            a, b, rows = place(-i, -j)
            form = 1 if b == 3 and a < 3 else 0
            copies.append(push(gm_v.at[e, form, rows], gg_v.at[e, a, b, rows],
                               h_send.at[2 * e + 1, n], h_recv.at[2 * e + 1, n], at(i, j)))
        return copies

    def spread_done(e, copies):
        for copy in copies:
            copy.wait_recv()
        for block in range(4):
            part = gg_v[e, block]
            if block == 3:
                part = part * edge_take[None]
            part = part.reshape(32, 256)
            high = part.astype(BF16)
            low = (part - high.astype(F32)).astype(BF16)
            mm_v[pl.ds(32 * block, 32), :] = high
            mm_v[pl.ds(128 + 32 * block, 32), :] = high
            ml_v[pl.ds(32 * block, 32), :] = low

    def picked(tile, r):
        return jnp.where(row == r, tile, 0.0).astype(BF16)

    def mixer(r):
        p, q, f = r // 4, (r // 2) % 2, r % 2
        return (mixh_v if f else mixl_v)[p, q]

    loads[0].wait()
    loads[1].wait()
    for copy in loads[2:]:
        copy.start()
    partial_start(0, x_v[...], None)
    pl.semaphore_wait(barrier, len(near))
    copies = partial_send(0)
    for k in range(1, nz):
        pl.semaphore_signal(hello, inc=1, device_id={"lat": at_z(k) * 2 + core},
                            device_id_type=MESH)

    loads[2].wait()
    loads[3].wait()
    ku_v[...] = kd_v[...].T
    xt_v[...] = x_v[...].T
    wt_v[...] = w_v[...].T
    loads[4].wait()
    loads[5].wait()
    loads[6].wait()

    coarse = partial_done(0, copies).astype(BF16).astype(F32)
    mixed = jnp.dot(picked(coarse, 0), mixer(0), preferred_element_type=F32)
    for r in range(1, 8):
        mixed = mixed + jnp.dot(picked(coarse, r), mixer(r), preferred_element_type=F32)
    copies = spread(0, mixed)
    spread_done(0, copies)

    bacc_v[...] = jnp.zeros_like(bacc_v)
    chunk = 256

    def gate(i, carry):
        rows = pl.ds(pl.multiple_of(i * chunk, chunk), chunk)
        pre = jnp.dot(ku_v[rows, :], mm_v[...], preferred_element_type=F32)
        pre = pre + jnp.dot(ku_v[rows, :128], ml_v[...], preferred_element_type=F32)
        pre = pre + jnp.dot(x_v[rows, :], w_v[...], preferred_element_type=F32)
        pre = pre + bias_v[...]
        cdf = 0.5 * (1.0 + lax.erf(pre * (1.0 / math.sqrt(2.0))))
        pdf = jnp.exp(-0.5 * pre * pre) * (1.0 / math.sqrt(2.0 * math.pi))
        grad = cot_v[rows, :].astype(F32) * (cdf + pre * pdf)
        high = grad.astype(BF16)
        ghi_v[rows, :] = high
        glo_v[rows, :] = (grad - high.astype(F32)).astype(BF16)
        bacc_v[...] += jnp.sum(grad.reshape(chunk // 8, 8, 256), axis=0)
        return carry

    lax.fori_loop(0, 1024 // chunk, gate, 0)

    total = jnp.dot(xt_v[...], ghi_v[...], preferred_element_type=F32)
    for h in range(2):
        cs_v[h] = total[:, h * 128 : (h + 1) * 128].reshape(nx, nz, tz, 8, 128)
    sem = iter(range(r_send.shape[0]))

    def send(src, dst, device):
        k = next(sem)
        return push(src, dst, r_send.at[k], r_recv.at[k], device)

    z_order = sorted(range(nz), key=lambda k: -min(k, nz - k))
    x_order = sorted(range(1, nx), key=lambda k: -min(k, nx - k))
    y_order = sorted(range(1, ny), key=lambda k: -min(k, ny - k))
    core_copies = [
        send(cs_v.at[1 - core, :, at_z(k)], cr_v.at[:, at_z(k)], partner) for k in z_order
    ]
    bias_sum = jnp.sum(bacc_v[...], axis=0, keepdims=True)
    bs_v[0, 0:1] = bias_sum[:, :128]
    bs_v[0, 1:2] = bias_sum[:, 128:]
    bias_core = send(bs_v.at[0], bc_v, partner)

    partial_start(1, ghi_v[...], glo_v[...])
    copies = partial_send(1)

    pl.semaphore_wait(hello, nz - 1)
    own_copies = []
    for n, k in enumerate(z_order):
        core_copies[n].wait_recv()
        zi = at_z(k)
        for j in x_order + [0]:
            xi = at_x(j)
            part = cs_v[core, xi, zi] + cr_v[xi, zi]
            if j == 0 and k == 0:
                rr_v[x, z] = part
            else:
                xs_v[j, k] = part
                own_copies.append(send(xs_v.at[j, k], rr_v.at[x, z], (zi * 2 + core, xi * ny + y)))

    def bias_spread(i, order, slot, device):
        bs_v[i] = bias_part
        br_v[i, slot] = bias_part
        return [send(bs_v.at[i], br_v.at[i, slot], device(k)) for k in order]

    def bias_add(i, count, waits):
        for copy in waits:
            copy.wait_recv()
        whole = br_v[i, 0]
        for j in range(1, count):
            whole = whole + br_v[i, j]
        return whole

    bias_core.wait_recv()
    bias_part = bs_v[0] + bc_v[...]
    bias_waits = bias_spread(1, x_order, x, lambda k: {"lon": at_x(k) * ny + y})

    back = partial_done(1, copies)
    bias_part = bias_add(1, nx, bias_waits)
    bias_waits = bias_spread(2, z_order[:-1], z, lambda k: {"lat": at_z(k) * 2 + core})
    back_rounded = back.astype(BF16).astype(F32)
    pull = None
    for r in range(8):
        term = lax.dot_general(picked(back_rounded, r), mixer(r), (((1,), (1,)), ((), ())),
                               preferred_element_type=F32)
        pull = term if pull is None else pull + term
    copies = spread(1, pull)

    for copy in own_copies:
        copy.wait_recv()
    columns = []
    for i in range(nx):
        red = rr_v[i, 0]
        for j in range(1, nz):
            red = red + rr_v[i, j]
        columns.append(red)
    red = columns[0]
    for column in columns[1:]:
        red = red + column
    ys_v[...] = red
    yr_v[y] = red
    y_copies = [send(ys_v, yr_v.at[y], {"lon": x * ny + at_y(k)}) for k in y_order]
    bias_part = bias_add(2, nz, bias_waits)
    bias_waits = bias_spread(3, y_order, y, lambda k: {"lon": x * ny + at_y(k)})

    columns = coarse.T
    for r in range(8):
        p, q, f = r // 4, (r // 2) % 2, r % 2
        outer = (columns[:, r : r + 1] * back[r : r + 1, :]).astype(BF16)
        (mhg_v if f else mlg_v)[p, q] = outer

    for copy in y_copies:
        copy.wait_recv()
    red = yr_v[0]
    for j in range(1, ny):
        red = red + yr_v[j]
    af_v[core, x, z] = red * (1.0 / math.sqrt(ncells))

    last = z_order[0]
    tile = af_v.at[core, x, z]
    arrivals = [
        send(tile, tile, (at_z(last) * 2 + 1 - core, at_x(j) * ny + y)) for j in x_order + [0]
    ]
    x_copies = {}
    for k in z_order:
        x_copies[k] = [
            send(tile, tile, (at_z(k) * 2 + core, at_x(j) * ny + y))
            for j in x_order + [0] if (j, k) != (0, 0)
        ]

    spread_done(1, copies)

    def back_out(i, carry):
        rows = pl.ds(pl.multiple_of(i * chunk, chunk), chunk)
        out = jnp.dot(ku_v[rows, :], mm_v[...], preferred_element_type=F32)
        out = out + jnp.dot(ku_v[rows, :128], ml_v[...], preferred_element_type=F32)
        out = out + jnp.dot(ghi_v[rows, :], wt_v[...], preferred_element_type=F32)
        fg_v[rows, :] = out.astype(BF16)
        return carry

    lax.fori_loop(0, 1024 // chunk, back_out, 0)

    for k in reversed(z_order[1:]):
        for copy in x_copies[k]:
            copy.wait_recv()
        column = af_v.at[core, :, lax.rem(z - k + nz, nz)]
        arrivals.append(send(column, column, partner))
    bg_v[...] = bias_add(3, ny, bias_waits) * (1.0 / math.sqrt(ncells))
    arrivals += x_copies[last]
    for copy in arrivals:
        copy.wait_recv()
    for copy in sends:
        copy.wait_send()


def leave(fg_v, mlg_v, mhg_v, af_v, bias_v, fg_hbm, mlg_hbm, mhg_hbm, wg_hbm, bg_hbm,
          wg_v, bg_v, sem):
    copies = [
        pltpu.make_async_copy(fg_v, fg_hbm, sem.at[0]),
        pltpu.make_async_copy(mlg_v, mlg_hbm, sem.at[1]),
        pltpu.make_async_copy(mhg_v, mhg_hbm, sem.at[2]),
        pltpu.make_async_copy(wg_v, wg_hbm, sem.at[3]),
        pltpu.make_async_copy(bg_v, bg_hbm, sem.at[4]),
    ]
    for copy in copies[:3]:
        copy.start()
    for h in range(2):
        wg_v[:, h * 128 : (h + 1) * 128] = af_v[h].reshape(256, 128)
        bg_v[:, h * 128 : (h + 1) * 128] = bias_v[h : h + 1]
    for copy in copies[3:]:
        copy.start()
    for copy in copies:
        copy.wait()


def shards(fields, cotangent, mix_low, mix_high, point_weight, point_bias):
    nlat, nlon = lax.axis_size("lat"), lax.axis_size("lon")
    rows, cols, channels = fields.shape
    cells = rows * cols
    tables = jnp.asarray(band_tables(rows * nlat, cols * nlon, rows, cols))
    nz, ny = nlat // 2, min(ROW, nlon // 2)
    nx = nlon // ny
    tx = 32 // nx
    tz = tx // nz
    messages = 2 * (nx * nz - 1) + nx + 2 * nz + (nx - 1) + (nz - 1) + 2 * (ny - 1)
    vmem = pltpu.VMEM
    scratch = [
        vmem((cells, channels), BF16), vmem((cells, channels), BF16),
        vmem(mix_low.shape, BF16), vmem(mix_high.shape, BF16),
        vmem((channels, channels), BF16), vmem((1, channels), F32), vmem((256, cells), BF16),
        vmem((cells, 256), BF16), vmem((channels, cells), BF16), vmem((channels, channels), BF16),
        vmem((cells, channels), BF16), vmem((cells, channels), BF16),
        vmem((256, channels), BF16), vmem((128, channels), BF16), vmem((8, channels), F32),
        vmem((2, 4, 4, 8, channels), F32), vmem((2, 4, 4, 8, channels), F32),
        vmem((2, 2, 8, channels), F32), vmem((2, 4, 4, 8, channels), F32),
        vmem((2, nx, nz, tz, 8, 128), F32), vmem((nx, nz, tz, 8, 128), F32),
        vmem((nx, nz, tz, 8, 128), F32), vmem((nx, nz, tz, 8, 128), F32),
        vmem((tz, 8, 128), F32), vmem((ny, tz, 8, 128), F32),
        vmem((4, 2, 128), F32), vmem((2, 128), F32), vmem((4, max(nx, ny, nz), 2, 128), F32),
        pltpu.SemaphoreType.DMA((7,)),
        pltpu.SemaphoreType.DMA((4, 24)), pltpu.SemaphoreType.DMA((4, 24)),
        pltpu.SemaphoreType.DMA((messages,)), pltpu.SemaphoreType.DMA((messages,)),
        pltpu.SemaphoreType.REGULAR,
    ]
    outs = pl.pallas_call(
        functools.partial(kernel, (nlat, nlon, cells * nlat * nlon)),
        out_shape=(
            jax.ShapeDtypeStruct((cells, channels), BF16),
            jax.ShapeDtypeStruct(mix_low.shape, BF16),
            jax.ShapeDtypeStruct(mix_high.shape, BF16),
            jax.ShapeDtypeStruct((2, nx, nz, tz, 8, 128), F32),
            jax.ShapeDtypeStruct((2, 128), F32),
        ),
        in_specs=[pl.BlockSpec(memory_space=pltpu.HBM)] * 7,
        out_specs=[pl.BlockSpec(memory_space=vmem)] * 5,
        scratch_shapes=scratch,
        compiler_params=pltpu.CompilerParams(
            collective_id=0, has_side_effects=True, vmem_limit_bytes=32 * 1024 * 1024
        ),
        name="wavelet_block",
    )(*[
        pltpu.with_memory_space_constraint(array, pltpu.HBM)
        for array in (
            fields.reshape(cells, channels), cotangent.reshape(cells, channels), mix_low, mix_high,
            point_weight, point_bias.reshape(1, channels), tables,
        )
    ])
    outs = pl.pallas_call(
        leave,
        out_shape=(
            jax.ShapeDtypeStruct((cells, channels), BF16),
            jax.ShapeDtypeStruct(mix_low.shape, BF16),
            jax.ShapeDtypeStruct(mix_high.shape, BF16),
            jax.ShapeDtypeStruct((channels, channels), F32),
            jax.ShapeDtypeStruct((1, channels), F32),
        ),
        in_specs=[pl.BlockSpec(memory_space=vmem)] * 5,
        out_specs=[pl.BlockSpec(memory_space=pltpu.HBM)] * 5,
        scratch_shapes=[
            vmem((channels, channels), F32), vmem((1, channels), F32),
            pltpu.SemaphoreType.DMA((5,)),
        ],
        compiler_params=pltpu.CompilerParams(vmem_limit_bytes=16 * 1024 * 1024),
        name="leave",
    )(outs[0], outs[1], outs[2], outs[3].reshape(2, 32, 8, 128), outs[4])
    return (
        outs[0].reshape(fields.shape), outs[1], outs[2], outs[3], outs[4].reshape(channels),
    )


def solution(mesh):
    placed = (
        P("lat", "lon", None),
        P("lat", "lon", None),
        P("lat", "lon", None, None),
        P("lat", "lon", None, None),
        P(),
        P(),
    )
    return jax.shard_map(
        shards,
        mesh=mesh,
        in_specs=placed,
        out_specs=(
            P("lat", "lon", None),
            P("lat", "lon", None, None),
            P("lat", "lon", None, None),
            P(),
            P(),
        ),
        check_vma=False,
    )
```

```python
import functools
import math

import jax
import jax.numpy as jnp
import numpy as np
from jax import lax
from jax.experimental import pallas as pl
from jax.experimental.pallas import tpu as pltpu
from jax.sharding import PartitionSpec as P

MESH = pl.DeviceIdType.MESH
F32 = jnp.float32
BF16 = jnp.bfloat16
ROW = 8

low_taps = (
    -0.010597401784997278,
    0.032883011666982945,
    0.030841381835986965,
    -0.18703481171888114,
    -0.02798376941698385,
    0.6308807679295904,
    0.7148465705525415,
    0.23037781330885523,
)
high_taps = (
    -0.23037781330885523,
    0.7148465705525415,
    -0.6308807679295904,
    -0.02798376941698385,
    0.18703481171888114,
    0.030841381835986965,
    -0.032883011666982945,
    -0.010597401784997278,
)


def level_matrix(count, taps, closed):
    matrix = np.zeros((count // 2, count))
    for k in range(count // 2):
        for j in range(8):
            n = 2 * k + j - 3
            if closed:
                matrix[k, n % count] += taps[j]
            elif 0 <= n < count:
                matrix[k, n] += taps[j]
    return matrix


def analysis_matrix(count, last_taps, closed):
    product = level_matrix(count, low_taps, closed)
    for level in (1, 2):
        product = level_matrix(count >> level, low_taps, closed) @ product
    return level_matrix(count >> 3, last_taps, closed) @ product


def coarse_offset(block, half):
    if block < 3:
        return 2 * (block - 1) + half
    return -3 if half == 1 else 4


def band_tables(nlat, nlon, band, sector):
    lat = analysis_matrix(nlat, low_taps, False)
    lons = [analysis_matrix(nlon, taps, True) for taps in (low_taps, high_taps)]
    bands = nlat // band
    tables = []
    for d in (0, bands // 2, bands - 1):
        rows = np.zeros((4, 2, band))
        for block in range(4):
            for p in range(2):
                k = 2 * d + coarse_offset(block, p)
                if 0 <= k < lat.shape[0]:
                    rows[block, p] = lat[k, d * band : (d + 1) * band]
        cols = np.zeros((4, 2, 2, sector))
        for block in range(4):
            for q in range(2):
                k = (2 + coarse_offset(block, q)) % lons[0].shape[0]
                for f in range(2):
                    cols[block, q, f] = lons[f][k, sector : 2 * sector]
        table = np.einsum("apn,bqfm->abpqfnm", rows, cols)
        table[:3, 3] = table[:3, 3].transpose(0, 2, 1, 3, 4, 5)
        tables.append(table.reshape(128, band * sector))
    full = np.stack(tables).astype(np.float32)
    high = full.astype(jnp.bfloat16)
    low = (full - high.astype(np.float32)).astype(jnp.bfloat16)
    return np.concatenate([high, low], axis=1)


def offsets():
    steps = [(i, j) for i in range(-2, 3) for j in range(-2, 3) if (i, j) != (0, 0)]
    return sorted(steps, key=lambda s: -(abs(s[1]) + abs(s[0]) / 2))


def place(i, j):
    a = 3 if abs(i) == 2 else i + 1
    b = 3 if abs(j) == 2 else j + 1
    start, size = 0, 8
    if a == 3 and b == 3:
        start, size = (4 if i < 0 else 0) + (2 if j < 0 else 0), 2
    elif a == 3:
        start, size = (4 if i < 0 else 0), 4
    elif b == 3:
        start, size = (4 if j < 0 else 0), 4
    return a, b, pl.ds(start, size)


def kernel(
    dims, x_hbm, cot_hbm, mixl_hbm, mixh_hbm, w_hbm, bias_hbm, k_hbm,
    fg_v, mlg_v, mhg_v, af_v, bg_v,
    x_v, cot_v, mixl_v, mixh_v, w_v, bias_v, kd_v,
    ku_v, xt_v, wt_v, ghi_v, glo_v, mm_v, ml_v, bacc_v,
    as_v, ar_v, gm_v, gg_v,
    cs_v, cr_v, xs_v, rr_v, ys_v, yr_v,
    bs_v, bc_v, br_v,
    in_sem, h_send, h_recv, r_send, r_recv, hello,
):
    nlat, nlon, ncells = dims
    nz, ny = nlat // 2, min(ROW, nlon // 2)
    nx = nlon // ny
    tx = 32 // nx
    tz = tx // nz
    lat, lon = lax.axis_index("lat"), lax.axis_index("lon")
    core, z = lax.rem(lat, 2), lat // 2
    y, x = lax.rem(lon, ny), lon // ny

    def at(i, j):
        return (lax.rem(lat + i + nlat, nlat), lax.rem(lon + j + nlon, nlon))

    other = lat + 1 - 2 * core
    partner = {"lat": other}

    def at_z(k):
        return lax.rem(z + k, nz)

    def at_x(k):
        return lax.rem(x + k, nx)

    def at_y(k):
        return lax.rem(y + k, ny)

    variant = (lat + nlat - 2) // (nlat - 1) + lat // (nlat - 1)
    loads = [
        (x_hbm, x_v), (k_hbm.at[variant], kd_v), (w_hbm, w_v), (bias_hbm, bias_v),
        (mixl_hbm, mixl_v), (mixh_hbm, mixh_v), (cot_hbm, cot_v),
    ]
    loads = [pltpu.make_async_copy(s, d, in_sem.at[i]) for i, (s, d) in enumerate(loads)]
    loads[0].start()

    barrier = pltpu.get_barrier_semaphore()
    near = [at(i, j) for i, j in offsets()]
    near += [{"lat": at_z(k) * 2 + core} for k in range(1, nz)]
    near += [(side, at_x(k) * ny + y) for k in range(1, nx) for side in (lat, other)]
    near += [{"lon": x * ny + at_y(k)} for k in range(1, ny)]
    for device in near:
        pl.semaphore_signal(barrier, inc=1, device_id=device, device_id_type=MESH)
    loads[1].start()

    sends = []

    def push(src, dst, send_sem, recv_sem, device):
        copy = pltpu.make_async_remote_copy(
            src_ref=src, dst_ref=dst, send_sem=send_sem, recv_sem=recv_sem,
            device_id=device, device_id_type=MESH,
        )
        copy.start()
        sends.append(copy)
        return copy

    row = lax.broadcasted_iota(jnp.int32, (8, 256), 0)
    below = jnp.where(lat >= 2, 1.0, 0.0)
    above = jnp.where(lat + 2 < nlat, 1.0, 0.0)
    edge_sum = jnp.where(row < 4, below, above)
    edge_take = jnp.where(row < 4, above, below)

    def swapped(tile):
        up, down = pltpu.roll(tile, 6, 0), pltpu.roll(tile, 2, 0)
        tile = jnp.where(row // 2 == 1, up, tile)
        return jnp.where(row // 2 == 2, down, tile)

    def partial_start(e, hi, lo):
        whole = jnp.dot(kd_v[...], hi, preferred_element_type=F32)
        part = whole[:128] + whole[128:]
        if lo is not None:
            part = part + jnp.dot(kd_v[:128], lo, preferred_element_type=F32)
        as_v[e] = part.reshape(4, 4, 8, 256)

    def partial_send(e):
        copies = []
        for n, (i, j) in enumerate(offsets()):
            spot = (e,) + place(i, j)
            copies.append(push(as_v.at[spot], ar_v.at[spot], h_send.at[2 * e, n],
                               h_recv.at[2 * e, n], at(i, j)))
        return copies

    def partial_done(e, copies):
        for copy in copies:
            copy.wait_recv()
        total = as_v[e, 1, 1]
        for a in range(3):
            for b in range(3):
                if (a, b) != (1, 1):
                    total = total + ar_v[e, a, b]
        far = (ar_v[e, 3, 0] + ar_v[e, 3, 1]) + (ar_v[e, 3, 2] + ar_v[e, 3, 3])
        side = ar_v[e, 0, 3] + ar_v[e, 1, 3] + ar_v[e, 2, 3]
        return total + far * edge_sum + swapped(side)

    def spread(e, tile):
        gm_v[e, 0] = tile
        gm_v[e, 1] = swapped(tile)
        gg_v[e, 1, 1] = tile
        copies = []
        for n, (i, j) in enumerate(offsets()):
            a, b, rows = place(-i, -j)
            form = 1 if b == 3 and a < 3 else 0
            copies.append(push(gm_v.at[e, form, rows], gg_v.at[e, a, b, rows],
                               h_send.at[2 * e + 1, n], h_recv.at[2 * e + 1, n], at(i, j)))
        return copies

    def spread_done(e, copies):
        for copy in copies:
            copy.wait_recv()
        for block in range(4):
            part = gg_v[e, block]
            if block == 3:
                part = part * edge_take[None]
            part = part.reshape(32, 256)
            high = part.astype(BF16)
            low = (part - high.astype(F32)).astype(BF16)
            mm_v[pl.ds(32 * block, 32), :] = high
            mm_v[pl.ds(128 + 32 * block, 32), :] = high
            ml_v[pl.ds(32 * block, 32), :] = low

    def picked(tile, r):
        return jnp.where(row == r, tile, 0.0).astype(BF16)

    def mixer(r):
        p, q, f = r // 4, (r // 2) % 2, r % 2
        return (mixh_v if f else mixl_v)[p, q]

    loads[0].wait()
    loads[1].wait()
    for copy in loads[2:]:
        copy.start()
    partial_start(0, x_v[...], None)
    pl.semaphore_wait(barrier, len(near))
    copies = partial_send(0)
    for k in range(1, nz):
        pl.semaphore_signal(hello, inc=1, device_id={"lat": at_z(k) * 2 + core},
                            device_id_type=MESH)

    loads[2].wait()
    loads[3].wait()
    ku_v[...] = kd_v[...].T
    xt_v[...] = x_v[...].T
    wt_v[...] = w_v[...].T
    loads[4].wait()
    loads[5].wait()
    loads[6].wait()

    coarse = partial_done(0, copies).astype(BF16).astype(F32)
    mixed = jnp.dot(picked(coarse, 0), mixer(0), preferred_element_type=F32)
    for r in range(1, 8):
        mixed = mixed + jnp.dot(picked(coarse, r), mixer(r), preferred_element_type=F32)
    copies = spread(0, mixed)
    spread_done(0, copies)

    bacc_v[...] = jnp.zeros_like(bacc_v)
    chunk = 256

    def gate(i, carry):
        rows = pl.ds(pl.multiple_of(i * chunk, chunk), chunk)
        pre = jnp.dot(ku_v[rows, :], mm_v[...], preferred_element_type=F32)
        pre = pre + jnp.dot(ku_v[rows, :128], ml_v[...], preferred_element_type=F32)
        pre = pre + jnp.dot(x_v[rows, :], w_v[...], preferred_element_type=F32)
        pre = pre + bias_v[...]
        cdf = 0.5 * (1.0 + lax.erf(pre * (1.0 / math.sqrt(2.0))))
        pdf = jnp.exp(-0.5 * pre * pre) * (1.0 / math.sqrt(2.0 * math.pi))
        grad = cot_v[rows, :].astype(F32) * (cdf + pre * pdf)
        high = grad.astype(BF16)
        ghi_v[rows, :] = high
        glo_v[rows, :] = (grad - high.astype(F32)).astype(BF16)
        bacc_v[...] += jnp.sum(grad.reshape(chunk // 8, 8, 256), axis=0)
        return carry

    lax.fori_loop(0, 1024 // chunk, gate, 0)

    total = jnp.dot(xt_v[...], ghi_v[...], preferred_element_type=F32)
    for h in range(2):
        cs_v[h] = total[:, h * 128 : (h + 1) * 128].reshape(nx, nz, tz, 8, 128)
    sem = iter(range(r_send.shape[0]))

    def send(src, dst, device):
        k = next(sem)
        return push(src, dst, r_send.at[k], r_recv.at[k], device)

    z_order = sorted(range(nz), key=lambda k: -min(k, nz - k))
    x_order = sorted(range(1, nx), key=lambda k: -min(k, nx - k))
    y_order = sorted(range(1, ny), key=lambda k: -min(k, ny - k))
    core_copies = [
        send(cs_v.at[1 - core, :, at_z(k)], cr_v.at[:, at_z(k)], partner) for k in z_order
    ]
    bias_sum = jnp.sum(bacc_v[...], axis=0, keepdims=True)
    bs_v[0, 0:1] = bias_sum[:, :128]
    bs_v[0, 1:2] = bias_sum[:, 128:]
    bias_core = send(bs_v.at[0], bc_v, partner)

    partial_start(1, ghi_v[...], glo_v[...])

    pl.semaphore_wait(hello, nz - 1)
    own_copies = []
    for n, k in enumerate(z_order):
        core_copies[n].wait_recv()
        zi = at_z(k)
        for j in x_order + [0]:
            xi = at_x(j)
            part = cs_v[core, xi, zi] + cr_v[xi, zi]
            if j == 0 and k == 0:
                rr_v[x, z] = part
            else:
                xs_v[j, k] = part
                own_copies.append(send(xs_v.at[j, k], rr_v.at[x, z], (zi * 2 + core, xi * ny + y)))

    copies = partial_send(1)

    def bias_spread(i, order, slot, device):
        bs_v[i] = bias_part
        br_v[i, slot] = bias_part
        return [send(bs_v.at[i], br_v.at[i, slot], device(k)) for k in order]

    def bias_add(i, count, waits):
        for copy in waits:
            copy.wait_recv()
        whole = br_v[i, 0]
        for j in range(1, count):
            whole = whole + br_v[i, j]
        return whole

    bias_core.wait_recv()
    bias_part = bs_v[0] + bc_v[...]
    bias_waits = bias_spread(1, x_order, x, lambda k: {"lon": at_x(k) * ny + y})

    for copy in own_copies:
        copy.wait_recv()
    columns = []
    for i in range(nx):
        red = rr_v[i, 0]
        for j in range(1, nz):
            red = red + rr_v[i, j]
        columns.append(red)
    red = columns[0]
    for column in columns[1:]:
        red = red + column
    ys_v[...] = red
    yr_v[y] = red
    y_copies = [send(ys_v, yr_v.at[y], {"lon": x * ny + at_y(k)}) for k in y_order]
    back = partial_done(1, copies)
    bias_part = bias_add(1, nx, bias_waits)
    bias_waits = bias_spread(2, z_order[:-1], z, lambda k: {"lat": at_z(k) * 2 + core})
    back_rounded = back.astype(BF16).astype(F32)
    pull = None
    for r in range(8):
        term = lax.dot_general(picked(back_rounded, r), mixer(r), (((1,), (1,)), ((), ())),
                               preferred_element_type=F32)
        pull = term if pull is None else pull + term
    copies = spread(1, pull)

    columns = coarse.T
    for r in range(8):
        p, q, f = r // 4, (r // 2) % 2, r % 2
        outer = (columns[:, r : r + 1] * back[r : r + 1, :]).astype(BF16)
        (mhg_v if f else mlg_v)[p, q] = outer

    for copy in y_copies:
        copy.wait_recv()
    red = yr_v[0]
    for j in range(1, ny):
        red = red + yr_v[j]
    af_v[core, x, z] = red * (1.0 / math.sqrt(ncells))

    last = z_order[0]
    tile = af_v.at[core, x, z]
    arrivals = [
        send(tile, tile, (at_z(last) * 2 + 1 - core, at_x(j) * ny + y)) for j in x_order + [0]
    ]
    x_copies = {}
    for k in z_order:
        x_copies[k] = [
            send(tile, tile, (at_z(k) * 2 + core, at_x(j) * ny + y))
            for j in x_order + [0] if (j, k) != (0, 0)
        ]

    bias_part = bias_add(2, nz, bias_waits)
    bias_waits = bias_spread(3, y_order, y, lambda k: {"lon": x * ny + at_y(k)})

    spread_done(1, copies)

    def back_out(i, carry):
        rows = pl.ds(pl.multiple_of(i * chunk, chunk), chunk)
        out = jnp.dot(ku_v[rows, :], mm_v[...], preferred_element_type=F32)
        out = out + jnp.dot(ku_v[rows, :128], ml_v[...], preferred_element_type=F32)
        out = out + jnp.dot(ghi_v[rows, :], wt_v[...], preferred_element_type=F32)
        fg_v[rows, :] = out.astype(BF16)
        return carry

    lax.fori_loop(0, 1024 // chunk, back_out, 0)

    for k in reversed(z_order[1:]):
        for copy in x_copies[k]:
            copy.wait_recv()
        column = af_v.at[core, :, lax.rem(z - k + nz, nz)]
        arrivals.append(send(column, column, partner))
    bg_v[...] = bias_add(3, ny, bias_waits) * (1.0 / math.sqrt(ncells))
    arrivals += x_copies[last]
    for copy in arrivals:
        copy.wait_recv()
    for copy in sends:
        copy.wait_send()


def leave(fg_v, mlg_v, mhg_v, af_v, bias_v, fg_hbm, mlg_hbm, mhg_hbm, wg_hbm, bg_hbm,
          wg_v, bg_v, sem):
    copies = [
        pltpu.make_async_copy(fg_v, fg_hbm, sem.at[0]),
        pltpu.make_async_copy(mlg_v, mlg_hbm, sem.at[1]),
        pltpu.make_async_copy(mhg_v, mhg_hbm, sem.at[2]),
        pltpu.make_async_copy(wg_v, wg_hbm, sem.at[3]),
        pltpu.make_async_copy(bg_v, bg_hbm, sem.at[4]),
    ]
    for copy in copies[:3]:
        copy.start()
    for h in range(2):
        wg_v[:, h * 128 : (h + 1) * 128] = af_v[h].reshape(256, 128)
        bg_v[:, h * 128 : (h + 1) * 128] = bias_v[h : h + 1]
    for copy in copies[3:]:
        copy.start()
    for copy in copies:
        copy.wait()


def shards(fields, cotangent, mix_low, mix_high, point_weight, point_bias):
    nlat, nlon = lax.axis_size("lat"), lax.axis_size("lon")
    rows, cols, channels = fields.shape
    cells = rows * cols
    tables = jnp.asarray(band_tables(rows * nlat, cols * nlon, rows, cols))
    nz, ny = nlat // 2, min(ROW, nlon // 2)
    nx = nlon // ny
    tx = 32 // nx
    tz = tx // nz
    messages = 2 * (nx * nz - 1) + nx + 2 * nz + (nx - 1) + (nz - 1) + 2 * (ny - 1)
    vmem = pltpu.VMEM
    scratch = [
        vmem((cells, channels), BF16), vmem((cells, channels), BF16),
        vmem(mix_low.shape, BF16), vmem(mix_high.shape, BF16),
        vmem((channels, channels), BF16), vmem((1, channels), F32), vmem((256, cells), BF16),
        vmem((cells, 256), BF16), vmem((channels, cells), BF16), vmem((channels, channels), BF16),
        vmem((cells, channels), BF16), vmem((cells, channels), BF16),
        vmem((256, channels), BF16), vmem((128, channels), BF16), vmem((8, channels), F32),
        vmem((2, 4, 4, 8, channels), F32), vmem((2, 4, 4, 8, channels), F32),
        vmem((2, 2, 8, channels), F32), vmem((2, 4, 4, 8, channels), F32),
        vmem((2, nx, nz, tz, 8, 128), F32), vmem((nx, nz, tz, 8, 128), F32),
        vmem((nx, nz, tz, 8, 128), F32), vmem((nx, nz, tz, 8, 128), F32),
        vmem((tz, 8, 128), F32), vmem((ny, tz, 8, 128), F32),
        vmem((4, 2, 128), F32), vmem((2, 128), F32), vmem((4, max(nx, ny, nz), 2, 128), F32),
        pltpu.SemaphoreType.DMA((7,)),
        pltpu.SemaphoreType.DMA((4, 24)), pltpu.SemaphoreType.DMA((4, 24)),
        pltpu.SemaphoreType.DMA((messages,)), pltpu.SemaphoreType.DMA((messages,)),
        pltpu.SemaphoreType.REGULAR,
    ]
    outs = pl.pallas_call(
        functools.partial(kernel, (nlat, nlon, cells * nlat * nlon)),
        out_shape=(
            jax.ShapeDtypeStruct((cells, channels), BF16),
            jax.ShapeDtypeStruct(mix_low.shape, BF16),
            jax.ShapeDtypeStruct(mix_high.shape, BF16),
            jax.ShapeDtypeStruct((2, nx, nz, tz, 8, 128), F32),
            jax.ShapeDtypeStruct((2, 128), F32),
        ),
        in_specs=[pl.BlockSpec(memory_space=pltpu.HBM)] * 7,
        out_specs=[pl.BlockSpec(memory_space=vmem)] * 5,
        scratch_shapes=scratch,
        compiler_params=pltpu.CompilerParams(
            collective_id=0, has_side_effects=True, vmem_limit_bytes=32 * 1024 * 1024
        ),
        name="wavelet_block",
    )(*[
        pltpu.with_memory_space_constraint(array, pltpu.HBM)
        for array in (
            fields.reshape(cells, channels), cotangent.reshape(cells, channels), mix_low, mix_high,
            point_weight, point_bias.reshape(1, channels), tables,
        )
    ])
    outs = pl.pallas_call(
        leave,
        out_shape=(
            jax.ShapeDtypeStruct((cells, channels), BF16),
            jax.ShapeDtypeStruct(mix_low.shape, BF16),
            jax.ShapeDtypeStruct(mix_high.shape, BF16),
            jax.ShapeDtypeStruct((channels, channels), F32),
            jax.ShapeDtypeStruct((1, channels), F32),
        ),
        in_specs=[pl.BlockSpec(memory_space=vmem)] * 5,
        out_specs=[pl.BlockSpec(memory_space=pltpu.HBM)] * 5,
        scratch_shapes=[
            vmem((channels, channels), F32), vmem((1, channels), F32),
            pltpu.SemaphoreType.DMA((5,)),
        ],
        compiler_params=pltpu.CompilerParams(vmem_limit_bytes=16 * 1024 * 1024),
        name="leave",
    )(outs[0], outs[1], outs[2], outs[3].reshape(2, 32, 8, 128), outs[4])
    return (
        outs[0].reshape(fields.shape), outs[1], outs[2], outs[3], outs[4].reshape(channels),
    )


def solution(mesh):
    placed = (
        P("lat", "lon", None),
        P("lat", "lon", None),
        P("lat", "lon", None, None),
        P("lat", "lon", None, None),
        P(),
        P(),
    )
    return jax.shard_map(
        shards,
        mesh=mesh,
        in_specs=placed,
        out_specs=(
            P("lat", "lon", None),
            P("lat", "lon", None, None),
            P("lat", "lon", None, None),
            P(),
            P(),
        ),
        check_vma=False,
    )
```

```python
import functools
import math

import jax
import jax.numpy as jnp
import numpy as np
from jax import lax
from jax.experimental import pallas as pl
from jax.experimental.pallas import tpu as pltpu
from jax.sharding import PartitionSpec as P

MESH = pl.DeviceIdType.MESH
F32 = jnp.float32
BF16 = jnp.bfloat16
ROW = 8

low_taps = (
    -0.010597401784997278,
    0.032883011666982945,
    0.030841381835986965,
    -0.18703481171888114,
    -0.02798376941698385,
    0.6308807679295904,
    0.7148465705525415,
    0.23037781330885523,
)
high_taps = (
    -0.23037781330885523,
    0.7148465705525415,
    -0.6308807679295904,
    -0.02798376941698385,
    0.18703481171888114,
    0.030841381835986965,
    -0.032883011666982945,
    -0.010597401784997278,
)


def level_matrix(count, taps, closed):
    matrix = np.zeros((count // 2, count))
    for k in range(count // 2):
        for j in range(8):
            n = 2 * k + j - 3
            if closed:
                matrix[k, n % count] += taps[j]
            elif 0 <= n < count:
                matrix[k, n] += taps[j]
    return matrix


def analysis_matrix(count, last_taps, closed):
    product = level_matrix(count, low_taps, closed)
    for level in (1, 2):
        product = level_matrix(count >> level, low_taps, closed) @ product
    return level_matrix(count >> 3, last_taps, closed) @ product


def coarse_offset(block, half):
    if block < 3:
        return 2 * (block - 1) + half
    return -3 if half == 1 else 4


def band_tables(nlat, nlon, band, sector):
    lat = analysis_matrix(nlat, low_taps, False)
    lons = [analysis_matrix(nlon, taps, True) for taps in (low_taps, high_taps)]
    bands = nlat // band
    tables = []
    for d in (0, bands // 2, bands - 1):
        rows = np.zeros((4, 2, band))
        for block in range(4):
            for p in range(2):
                k = 2 * d + coarse_offset(block, p)
                if 0 <= k < lat.shape[0]:
                    rows[block, p] = lat[k, d * band : (d + 1) * band]
        cols = np.zeros((4, 2, 2, sector))
        for block in range(4):
            for q in range(2):
                k = (2 + coarse_offset(block, q)) % lons[0].shape[0]
                for f in range(2):
                    cols[block, q, f] = lons[f][k, sector : 2 * sector]
        table = np.einsum("apn,bqfm->abpqfnm", rows, cols)
        table[:3, 3] = table[:3, 3].transpose(0, 2, 1, 3, 4, 5)
        tables.append(table.reshape(128, band * sector))
    full = np.stack(tables).astype(np.float32)
    high = full.astype(jnp.bfloat16)
    low = (full - high.astype(np.float32)).astype(jnp.bfloat16)
    return np.concatenate([high, low], axis=1)


def offsets():
    steps = [(i, j) for i in range(-2, 3) for j in range(-2, 3) if (i, j) != (0, 0)]
    return sorted(steps, key=lambda s: -(abs(s[1]) + abs(s[0]) / 2))


def place(i, j):
    a = 3 if abs(i) == 2 else i + 1
    b = 3 if abs(j) == 2 else j + 1
    start, size = 0, 8
    if a == 3 and b == 3:
        start, size = (4 if i < 0 else 0) + (2 if j < 0 else 0), 2
    elif a == 3:
        start, size = (4 if i < 0 else 0), 4
    elif b == 3:
        start, size = (4 if j < 0 else 0), 4
    return a, b, pl.ds(start, size)


def kernel(
    dims, x_hbm, cot_hbm, mixl_hbm, mixh_hbm, w_hbm, bias_hbm, k_hbm,
    fg_v, mlg_v, mhg_v, af_v, bg_v,
    x_v, cot_v, mixl_v, mixh_v, w_v, bias_v, kd_v,
    ku_v, xt_v, wt_v, ghi_v, glo_v, mm_v, ml_v, bacc_v,
    as_v, ar_v, gm_v, gg_v,
    cs_v, cr_v, xs_v, rr_v, ys_v, yr_v,
    bs_v, bc_v, br_v,
    in_sem, h_send, h_recv, r_send, r_recv, hello,
):
    nlat, nlon, ncells = dims
    nz, ny = nlat // 2, min(ROW, nlon // 2)
    nx = nlon // ny
    tx = 32 // nx
    tz = tx // nz
    lat, lon = lax.axis_index("lat"), lax.axis_index("lon")
    core, z = lax.rem(lat, 2), lat // 2
    y, x = lax.rem(lon, ny), lon // ny

    def at(i, j):
        return (lax.rem(lat + i + nlat, nlat), lax.rem(lon + j + nlon, nlon))

    other = lat + 1 - 2 * core
    partner = {"lat": other}

    def at_z(k):
        return lax.rem(z + k, nz)

    def at_x(k):
        return lax.rem(x + k, nx)

    def at_y(k):
        return lax.rem(y + k, ny)

    variant = (lat + nlat - 2) // (nlat - 1) + lat // (nlat - 1)
    loads = [
        (x_hbm, x_v), (k_hbm.at[variant], kd_v), (w_hbm, w_v), (bias_hbm, bias_v),
        (mixl_hbm, mixl_v), (mixh_hbm, mixh_v), (cot_hbm, cot_v),
    ]
    loads = [pltpu.make_async_copy(s, d, in_sem.at[i]) for i, (s, d) in enumerate(loads)]
    loads[0].start()

    barrier = pltpu.get_barrier_semaphore()
    near = [at(i, j) for i, j in offsets()]
    near += [{"lat": at_z(k) * 2 + core} for k in range(1, nz)]
    near += [(side, at_x(k) * ny + y) for k in range(1, nx) for side in (lat, other)]
    near += [{"lon": x * ny + at_y(k)} for k in range(1, ny)]
    for device in near:
        pl.semaphore_signal(barrier, inc=1, device_id=device, device_id_type=MESH)
    loads[1].start()

    sends = []

    def push(src, dst, send_sem, recv_sem, device):
        copy = pltpu.make_async_remote_copy(
            src_ref=src, dst_ref=dst, send_sem=send_sem, recv_sem=recv_sem,
            device_id=device, device_id_type=MESH,
        )
        copy.start()
        sends.append(copy)
        return copy

    row = lax.broadcasted_iota(jnp.int32, (8, 256), 0)
    below = jnp.where(lat >= 2, 1.0, 0.0)
    above = jnp.where(lat + 2 < nlat, 1.0, 0.0)
    edge_sum = jnp.where(row < 4, below, above)
    edge_take = jnp.where(row < 4, above, below)

    def swapped(tile):
        up, down = pltpu.roll(tile, 6, 0), pltpu.roll(tile, 2, 0)
        tile = jnp.where(row // 2 == 1, up, tile)
        return jnp.where(row // 2 == 2, down, tile)

    def partial_start(e, hi, lo):
        whole = jnp.dot(kd_v[...], hi, preferred_element_type=F32)
        part = whole[:128] + whole[128:]
        if lo is not None:
            part = part + jnp.dot(kd_v[:128], lo, preferred_element_type=F32)
        as_v[e] = part.reshape(4, 4, 8, 256)

    def partial_send(e):
        copies = []
        for n, (i, j) in enumerate(offsets()):
            spot = (e,) + place(i, j)
            copies.append(push(as_v.at[spot], ar_v.at[spot], h_send.at[2 * e, n],
                               h_recv.at[2 * e, n], at(i, j)))
        return copies

    def partial_done(e, copies):
        for copy in copies:
            copy.wait_recv()
        total = as_v[e, 1, 1]
        for a in range(3):
            for b in range(3):
                if (a, b) != (1, 1):
                    total = total + ar_v[e, a, b]
        far = (ar_v[e, 3, 0] + ar_v[e, 3, 1]) + (ar_v[e, 3, 2] + ar_v[e, 3, 3])
        side = ar_v[e, 0, 3] + ar_v[e, 1, 3] + ar_v[e, 2, 3]
        return total + far * edge_sum + swapped(side)

    def spread(e, tile):
        gm_v[e, 0] = tile
        gm_v[e, 1] = swapped(tile)
        gg_v[e, 1, 1] = tile
        copies = []
        for n, (i, j) in enumerate(offsets()):
            a, b, rows = place(-i, -j)
            form = 1 if b == 3 and a < 3 else 0
            copies.append(push(gm_v.at[e, form, rows], gg_v.at[e, a, b, rows],
                               h_send.at[2 * e + 1, n], h_recv.at[2 * e + 1, n], at(i, j)))
        return copies

    def spread_done(e, copies):
        for copy in copies:
            copy.wait_recv()
        for block in range(4):
            part = gg_v[e, block]
            if block == 3:
                part = part * edge_take[None]
            part = part.reshape(32, 256)
            high = part.astype(BF16)
            low = (part - high.astype(F32)).astype(BF16)
            mm_v[pl.ds(32 * block, 32), :] = high
            mm_v[pl.ds(128 + 32 * block, 32), :] = high
            ml_v[pl.ds(32 * block, 32), :] = low

    def picked(tile, r):
        return jnp.where(row == r, tile, 0.0).astype(BF16)

    def mixer(r):
        p, q, f = r // 4, (r // 2) % 2, r % 2
        return (mixh_v if f else mixl_v)[p, q]

    loads[0].wait()
    loads[1].wait()
    for copy in loads[2:]:
        copy.start()
    partial_start(0, x_v[...], None)
    pl.semaphore_wait(barrier, len(near))
    copies = partial_send(0)
    for k in range(1, nz):
        pl.semaphore_signal(hello, inc=1, device_id={"lat": at_z(k) * 2 + core},
                            device_id_type=MESH)

    loads[2].wait()
    loads[3].wait()
    ku_v[...] = kd_v[...].T
    xt_v[...] = x_v[...].T
    wt_v[...] = w_v[...].T
    loads[4].wait()
    loads[5].wait()
    loads[6].wait()

    coarse = partial_done(0, copies).astype(BF16).astype(F32)
    mixed = jnp.dot(picked(coarse, 0), mixer(0), preferred_element_type=F32)
    for r in range(1, 8):
        mixed = mixed + jnp.dot(picked(coarse, r), mixer(r), preferred_element_type=F32)
    copies = spread(0, mixed)
    spread_done(0, copies)

    bacc_v[...] = jnp.zeros_like(bacc_v)
    chunk = 256

    def gate_half(h):
        lane = pl.ds(pl.multiple_of(h * 128, 128), 128)

        def gate(i, carry):
            rows = pl.ds(pl.multiple_of(i * chunk, chunk), chunk)
            pre = jnp.dot(ku_v[rows, :], mm_v[:, lane], preferred_element_type=F32)
            pre = pre + jnp.dot(ku_v[rows, :128], ml_v[:, lane], preferred_element_type=F32)
            pre = pre + jnp.dot(x_v[rows, :], w_v[:, lane], preferred_element_type=F32)
            pre = pre + bias_v[:, lane]
            cdf = 0.5 * (1.0 + lax.erf(pre * (1.0 / math.sqrt(2.0))))
            pdf = jnp.exp(-0.5 * pre * pre) * (1.0 / math.sqrt(2.0 * math.pi))
            grad = cot_v[rows, lane].astype(F32) * (cdf + pre * pdf)
            high = grad.astype(BF16)
            ghi_v[rows, lane] = high
            glo_v[rows, lane] = (grad - high.astype(F32)).astype(BF16)
            bacc_v[:, lane] += jnp.sum(grad.reshape(chunk // 8, 8, 128), axis=0)
            return carry

        lax.fori_loop(0, 1024 // chunk, gate, 0)
        total = jnp.dot(xt_v[...], ghi_v[:, lane], preferred_element_type=F32)
        cs_v[h] = total.reshape(nx, nz, tz, 8, 128)

    gate_half(1 - core)
    sem = iter(range(r_send.shape[0]))

    def send(src, dst, device):
        k = next(sem)
        return push(src, dst, r_send.at[k], r_recv.at[k], device)

    z_order = sorted(range(nz), key=lambda k: -min(k, nz - k))
    x_order = sorted(range(1, nx), key=lambda k: -min(k, nx - k))
    y_order = sorted(range(1, ny), key=lambda k: -min(k, ny - k))
    core_copies = [
        send(cs_v.at[1 - core, :, at_z(k)], cr_v.at[:, at_z(k)], partner) for k in z_order
    ]
    gate_half(core)
    bias_sum = jnp.sum(bacc_v[...], axis=0, keepdims=True)
    bs_v[0, 0:1] = bias_sum[:, :128]
    bs_v[0, 1:2] = bias_sum[:, 128:]
    bias_core = send(bs_v.at[0], bc_v, partner)


    pl.semaphore_wait(hello, nz - 1)
    own_copies = []
    for n, k in enumerate(z_order):
        core_copies[n].wait_recv()
        zi = at_z(k)
        for j in x_order + [0]:
            xi = at_x(j)
            part = cs_v[core, xi, zi] + cr_v[xi, zi]
            if j == 0 and k == 0:
                rr_v[x, z] = part
            else:
                xs_v[j, k] = part
                own_copies.append(send(xs_v.at[j, k], rr_v.at[x, z], (zi * 2 + core, xi * ny + y)))

    partial_start(1, ghi_v[...], glo_v[...])
    copies = partial_send(1)

    def bias_spread(i, order, slot, device):
        bs_v[i] = bias_part
        br_v[i, slot] = bias_part
        return [send(bs_v.at[i], br_v.at[i, slot], device(k)) for k in order]

    def bias_add(i, count, waits):
        for copy in waits:
            copy.wait_recv()
        whole = br_v[i, 0]
        for j in range(1, count):
            whole = whole + br_v[i, j]
        return whole

    bias_core.wait_recv()
    bias_part = bs_v[0] + bc_v[...]
    bias_waits = bias_spread(1, x_order, x, lambda k: {"lon": at_x(k) * ny + y})

    for copy in own_copies:
        copy.wait_recv()
    columns = []
    for i in range(nx):
        red = rr_v[i, 0]
        for j in range(1, nz):
            red = red + rr_v[i, j]
        columns.append(red)
    red = columns[0]
    for column in columns[1:]:
        red = red + column
    ys_v[...] = red
    yr_v[y] = red
    y_copies = [send(ys_v, yr_v.at[y], {"lon": x * ny + at_y(k)}) for k in y_order]
    back = partial_done(1, copies)
    bias_part = bias_add(1, nx, bias_waits)
    bias_waits = bias_spread(2, z_order[:-1], z, lambda k: {"lat": at_z(k) * 2 + core})
    back_rounded = back.astype(BF16).astype(F32)
    pull = None
    for r in range(8):
        term = lax.dot_general(picked(back_rounded, r), mixer(r), (((1,), (1,)), ((), ())),
                               preferred_element_type=F32)
        pull = term if pull is None else pull + term
    copies = spread(1, pull)

    columns = coarse.T
    for r in range(8):
        p, q, f = r // 4, (r // 2) % 2, r % 2
        outer = (columns[:, r : r + 1] * back[r : r + 1, :]).astype(BF16)
        (mhg_v if f else mlg_v)[p, q] = outer

    for copy in y_copies:
        copy.wait_recv()
    red = yr_v[0]
    for j in range(1, ny):
        red = red + yr_v[j]
    af_v[core, x, z] = red * (1.0 / math.sqrt(ncells))

    last = z_order[0]
    tile = af_v.at[core, x, z]
    arrivals = [
        send(tile, tile, (at_z(last) * 2 + 1 - core, at_x(j) * ny + y)) for j in x_order + [0]
    ]
    x_copies = {}
    for k in z_order:
        x_copies[k] = [
            send(tile, tile, (at_z(k) * 2 + core, at_x(j) * ny + y))
            for j in x_order + [0] if (j, k) != (0, 0)
        ]

    bias_part = bias_add(2, nz, bias_waits)
    bias_waits = bias_spread(3, y_order, y, lambda k: {"lon": x * ny + at_y(k)})

    spread_done(1, copies)

    def back_out(i, carry):
        rows = pl.ds(pl.multiple_of(i * chunk, chunk), chunk)
        out = jnp.dot(ku_v[rows, :], mm_v[...], preferred_element_type=F32)
        out = out + jnp.dot(ku_v[rows, :128], ml_v[...], preferred_element_type=F32)
        out = out + jnp.dot(ghi_v[rows, :], wt_v[...], preferred_element_type=F32)
        fg_v[rows, :] = out.astype(BF16)
        return carry

    lax.fori_loop(0, 1024 // chunk, back_out, 0)

    for k in reversed(z_order[1:]):
        for copy in x_copies[k]:
            copy.wait_recv()
        column = af_v.at[core, :, lax.rem(z - k + nz, nz)]
        arrivals.append(send(column, column, partner))
    bg_v[...] = bias_add(3, ny, bias_waits) * (1.0 / math.sqrt(ncells))
    arrivals += x_copies[last]
    for copy in arrivals:
        copy.wait_recv()
    for copy in sends:
        copy.wait_send()


def leave(fg_v, mlg_v, mhg_v, af_v, bias_v, fg_hbm, mlg_hbm, mhg_hbm, wg_hbm, bg_hbm,
          wg_v, bg_v, sem):
    copies = [
        pltpu.make_async_copy(fg_v, fg_hbm, sem.at[0]),
        pltpu.make_async_copy(mlg_v, mlg_hbm, sem.at[1]),
        pltpu.make_async_copy(mhg_v, mhg_hbm, sem.at[2]),
        pltpu.make_async_copy(wg_v, wg_hbm, sem.at[3]),
        pltpu.make_async_copy(bg_v, bg_hbm, sem.at[4]),
    ]
    for copy in copies[:3]:
        copy.start()
    for h in range(2):
        wg_v[:, h * 128 : (h + 1) * 128] = af_v[h].reshape(256, 128)
        bg_v[:, h * 128 : (h + 1) * 128] = bias_v[h : h + 1]
    for copy in copies[3:]:
        copy.start()
    for copy in copies:
        copy.wait()


def shards(fields, cotangent, mix_low, mix_high, point_weight, point_bias):
    nlat, nlon = lax.axis_size("lat"), lax.axis_size("lon")
    rows, cols, channels = fields.shape
    cells = rows * cols
    tables = jnp.asarray(band_tables(rows * nlat, cols * nlon, rows, cols))
    nz, ny = nlat // 2, min(ROW, nlon // 2)
    nx = nlon // ny
    tx = 32 // nx
    tz = tx // nz
    messages = 2 * (nx * nz - 1) + nx + 2 * nz + (nx - 1) + (nz - 1) + 2 * (ny - 1)
    vmem = pltpu.VMEM
    scratch = [
        vmem((cells, channels), BF16), vmem((cells, channels), BF16),
        vmem(mix_low.shape, BF16), vmem(mix_high.shape, BF16),
        vmem((channels, channels), BF16), vmem((1, channels), F32), vmem((256, cells), BF16),
        vmem((cells, 256), BF16), vmem((channels, cells), BF16), vmem((channels, channels), BF16),
        vmem((cells, channels), BF16), vmem((cells, channels), BF16),
        vmem((256, channels), BF16), vmem((128, channels), BF16), vmem((8, channels), F32),
        vmem((2, 4, 4, 8, channels), F32), vmem((2, 4, 4, 8, channels), F32),
        vmem((2, 2, 8, channels), F32), vmem((2, 4, 4, 8, channels), F32),
        vmem((2, nx, nz, tz, 8, 128), F32), vmem((nx, nz, tz, 8, 128), F32),
        vmem((nx, nz, tz, 8, 128), F32), vmem((nx, nz, tz, 8, 128), F32),
        vmem((tz, 8, 128), F32), vmem((ny, tz, 8, 128), F32),
        vmem((4, 2, 128), F32), vmem((2, 128), F32), vmem((4, max(nx, ny, nz), 2, 128), F32),
        pltpu.SemaphoreType.DMA((7,)),
        pltpu.SemaphoreType.DMA((4, 24)), pltpu.SemaphoreType.DMA((4, 24)),
        pltpu.SemaphoreType.DMA((messages,)), pltpu.SemaphoreType.DMA((messages,)),
        pltpu.SemaphoreType.REGULAR,
    ]
    outs = pl.pallas_call(
        functools.partial(kernel, (nlat, nlon, cells * nlat * nlon)),
        out_shape=(
            jax.ShapeDtypeStruct((cells, channels), BF16),
            jax.ShapeDtypeStruct(mix_low.shape, BF16),
            jax.ShapeDtypeStruct(mix_high.shape, BF16),
            jax.ShapeDtypeStruct((2, nx, nz, tz, 8, 128), F32),
            jax.ShapeDtypeStruct((2, 128), F32),
        ),
        in_specs=[pl.BlockSpec(memory_space=pltpu.HBM)] * 7,
        out_specs=[pl.BlockSpec(memory_space=vmem)] * 5,
        scratch_shapes=scratch,
        compiler_params=pltpu.CompilerParams(
            collective_id=0, has_side_effects=True, vmem_limit_bytes=32 * 1024 * 1024
        ),
        name="wavelet_block",
    )(*[
        pltpu.with_memory_space_constraint(array, pltpu.HBM)
        for array in (
            fields.reshape(cells, channels), cotangent.reshape(cells, channels), mix_low, mix_high,
            point_weight, point_bias.reshape(1, channels), tables,
        )
    ])
    outs = pl.pallas_call(
        leave,
        out_shape=(
            jax.ShapeDtypeStruct((cells, channels), BF16),
            jax.ShapeDtypeStruct(mix_low.shape, BF16),
            jax.ShapeDtypeStruct(mix_high.shape, BF16),
            jax.ShapeDtypeStruct((channels, channels), F32),
            jax.ShapeDtypeStruct((1, channels), F32),
        ),
        in_specs=[pl.BlockSpec(memory_space=vmem)] * 5,
        out_specs=[pl.BlockSpec(memory_space=pltpu.HBM)] * 5,
        scratch_shapes=[
            vmem((channels, channels), F32), vmem((1, channels), F32),
            pltpu.SemaphoreType.DMA((5,)),
        ],
        compiler_params=pltpu.CompilerParams(vmem_limit_bytes=16 * 1024 * 1024),
        name="leave",
    )(outs[0], outs[1], outs[2], outs[3].reshape(2, 32, 8, 128), outs[4])
    return (
        outs[0].reshape(fields.shape), outs[1], outs[2], outs[3], outs[4].reshape(channels),
    )


def solution(mesh):
    placed = (
        P("lat", "lon", None),
        P("lat", "lon", None),
        P("lat", "lon", None, None),
        P("lat", "lon", None, None),
        P(),
        P(),
    )
    return jax.shard_map(
        shards,
        mesh=mesh,
        in_specs=placed,
        out_specs=(
            P("lat", "lon", None),
            P("lat", "lon", None, None),
            P("lat", "lon", None, None),
            P(),
            P(),
        ),
        check_vma=False,
    )
```

```python
import functools
import math

import jax
import jax.numpy as jnp
import numpy as np
from jax import lax
from jax.experimental import pallas as pl
from jax.experimental.pallas import tpu as pltpu
from jax.sharding import PartitionSpec as P

MESH = pl.DeviceIdType.MESH
F32 = jnp.float32
BF16 = jnp.bfloat16
ROW = 8

low_taps = (
    -0.010597401784997278,
    0.032883011666982945,
    0.030841381835986965,
    -0.18703481171888114,
    -0.02798376941698385,
    0.6308807679295904,
    0.7148465705525415,
    0.23037781330885523,
)
high_taps = (
    -0.23037781330885523,
    0.7148465705525415,
    -0.6308807679295904,
    -0.02798376941698385,
    0.18703481171888114,
    0.030841381835986965,
    -0.032883011666982945,
    -0.010597401784997278,
)


def level_matrix(count, taps, closed):
    matrix = np.zeros((count // 2, count))
    for k in range(count // 2):
        for j in range(8):
            n = 2 * k + j - 3
            if closed:
                matrix[k, n % count] += taps[j]
            elif 0 <= n < count:
                matrix[k, n] += taps[j]
    return matrix


def analysis_matrix(count, last_taps, closed):
    product = level_matrix(count, low_taps, closed)
    for level in (1, 2):
        product = level_matrix(count >> level, low_taps, closed) @ product
    return level_matrix(count >> 3, last_taps, closed) @ product


def coarse_offset(block, half):
    if block < 3:
        return 2 * (block - 1) + half
    return -3 if half == 1 else 4


def band_tables(nlat, nlon, band, sector):
    lat = analysis_matrix(nlat, low_taps, False)
    lons = [analysis_matrix(nlon, taps, True) for taps in (low_taps, high_taps)]
    bands = nlat // band
    tables = []
    for d in (0, bands // 2, bands - 1):
        rows = np.zeros((4, 2, band))
        for block in range(4):
            for p in range(2):
                k = 2 * d + coarse_offset(block, p)
                if 0 <= k < lat.shape[0]:
                    rows[block, p] = lat[k, d * band : (d + 1) * band]
        cols = np.zeros((4, 2, 2, sector))
        for block in range(4):
            for q in range(2):
                k = (2 + coarse_offset(block, q)) % lons[0].shape[0]
                for f in range(2):
                    cols[block, q, f] = lons[f][k, sector : 2 * sector]
        table = np.einsum("apn,bqfm->abpqfnm", rows, cols)
        table[:3, 3] = table[:3, 3].transpose(0, 2, 1, 3, 4, 5)
        tables.append(table.reshape(128, band * sector))
    full = np.stack(tables).astype(np.float32)
    high = full.astype(jnp.bfloat16)
    low = (full - high.astype(np.float32)).astype(jnp.bfloat16)
    return np.concatenate([high, low], axis=1)


def offsets():
    steps = [(i, j) for i in range(-2, 3) for j in range(-2, 3) if (i, j) != (0, 0)]
    return sorted(steps, key=lambda s: -(abs(s[1]) + abs(s[0]) / 2))


def place(i, j):
    a = 3 if abs(i) == 2 else i + 1
    b = 3 if abs(j) == 2 else j + 1
    start, size = 0, 8
    if a == 3 and b == 3:
        start, size = (4 if i < 0 else 0) + (2 if j < 0 else 0), 2
    elif a == 3:
        start, size = (4 if i < 0 else 0), 4
    elif b == 3:
        start, size = (4 if j < 0 else 0), 4
    return a, b, pl.ds(start, size)


def kernel(
    dims, x_hbm, cot_hbm, mixl_hbm, mixh_hbm, w_hbm, bias_hbm, k_hbm,
    fg_v, mlg_v, mhg_v, af_v, bg_v,
    x_v, cot_v, mixl_v, mixh_v, w_v, bias_v, kd_v,
    ku_v, xt_v, wt_v, ghi_v, glo_v, mm_v, ml_v, bacc_v,
    as_v, ar_v, gm_v, gg_v,
    cs_v, cr_v, xs_v, rr_v, ys_v, yr_v,
    bs_v, bc_v, br_v,
    in_sem, h_send, h_recv, r_send, r_recv, hello,
):
    nlat, nlon, ncells = dims
    nz, ny = nlat // 2, min(ROW, nlon // 2)
    nx = nlon // ny
    tx = 32 // nx
    tz = tx // nz
    lat, lon = lax.axis_index("lat"), lax.axis_index("lon")
    core, z = lax.rem(lat, 2), lat // 2
    y, x = lax.rem(lon, ny), lon // ny

    def at(i, j):
        return (lax.rem(lat + i + nlat, nlat), lax.rem(lon + j + nlon, nlon))

    other = lat + 1 - 2 * core
    partner = {"lat": other}

    def at_z(k):
        return lax.rem(z + k, nz)

    def at_x(k):
        return lax.rem(x + k, nx)

    def at_y(k):
        return lax.rem(y + k, ny)

    variant = (lat + nlat - 2) // (nlat - 1) + lat // (nlat - 1)
    loads = [
        (x_hbm, x_v), (k_hbm.at[variant], kd_v), (w_hbm, w_v), (bias_hbm, bias_v),
        (mixl_hbm, mixl_v), (mixh_hbm, mixh_v), (cot_hbm, cot_v),
    ]
    loads = [pltpu.make_async_copy(s, d, in_sem.at[i]) for i, (s, d) in enumerate(loads)]
    loads[0].start()

    barrier = pltpu.get_barrier_semaphore()
    near = [at(i, j) for i, j in offsets()]
    near += [{"lat": at_z(k) * 2 + core} for k in range(1, nz)]
    near += [(side, at_x(k) * ny + y) for k in range(1, nx) for side in (lat, other)]
    near += [{"lon": x * ny + at_y(k)} for k in range(1, ny)]
    for device in near:
        pl.semaphore_signal(barrier, inc=1, device_id=device, device_id_type=MESH)
    loads[1].start()

    sends = []

    def push(src, dst, send_sem, recv_sem, device):
        copy = pltpu.make_async_remote_copy(
            src_ref=src, dst_ref=dst, send_sem=send_sem, recv_sem=recv_sem,
            device_id=device, device_id_type=MESH,
        )
        copy.start()
        sends.append(copy)
        return copy

    row = lax.broadcasted_iota(jnp.int32, (8, 256), 0)
    below = jnp.where(lat >= 2, 1.0, 0.0)
    above = jnp.where(lat + 2 < nlat, 1.0, 0.0)
    edge_sum = jnp.where(row < 4, below, above)
    edge_take = jnp.where(row < 4, above, below)

    def swapped(tile):
        up, down = pltpu.roll(tile, 6, 0), pltpu.roll(tile, 2, 0)
        tile = jnp.where(row // 2 == 1, up, tile)
        return jnp.where(row // 2 == 2, down, tile)

    def partial_start(e, hi, lo):
        whole = jnp.dot(kd_v[...], hi, preferred_element_type=F32)
        part = whole[:128] + whole[128:]
        if lo is not None:
            part = part + jnp.dot(kd_v[:128], lo, preferred_element_type=F32)
        as_v[e] = part.reshape(4, 4, 8, 256)

    def partial_send(e):
        copies = []
        for n, (i, j) in enumerate(offsets()):
            spot = (e,) + place(i, j)
            copies.append(push(as_v.at[spot], ar_v.at[spot], h_send.at[2 * e, n],
                               h_recv.at[2 * e, n], at(i, j)))
        return copies

    def partial_done(e, copies):
        for copy in copies:
            copy.wait_recv()
        total = as_v[e, 1, 1]
        for a in range(3):
            for b in range(3):
                if (a, b) != (1, 1):
                    total = total + ar_v[e, a, b]
        far = (ar_v[e, 3, 0] + ar_v[e, 3, 1]) + (ar_v[e, 3, 2] + ar_v[e, 3, 3])
        side = ar_v[e, 0, 3] + ar_v[e, 1, 3] + ar_v[e, 2, 3]
        return total + far * edge_sum + swapped(side)

    def spread(e, tile):
        gm_v[e, 0] = tile
        gm_v[e, 1] = swapped(tile)
        gg_v[e, 1, 1] = tile
        copies = []
        for n, (i, j) in enumerate(offsets()):
            a, b, rows = place(-i, -j)
            form = 1 if b == 3 and a < 3 else 0
            copies.append(push(gm_v.at[e, form, rows], gg_v.at[e, a, b, rows],
                               h_send.at[2 * e + 1, n], h_recv.at[2 * e + 1, n], at(i, j)))
        return copies

    def spread_done(e, copies):
        for copy in copies:
            copy.wait_recv()
        for block in range(4):
            part = gg_v[e, block]
            if block == 3:
                part = part * edge_take[None]
            part = part.reshape(32, 256)
            high = part.astype(BF16)
            low = (part - high.astype(F32)).astype(BF16)
            mm_v[pl.ds(32 * block, 32), :] = high
            mm_v[pl.ds(128 + 32 * block, 32), :] = high
            ml_v[pl.ds(32 * block, 32), :] = low

    def picked(tile, r):
        return jnp.where(row == r, tile, 0.0).astype(BF16)

    def mixer(r):
        p, q, f = r // 4, (r // 2) % 2, r % 2
        return (mixh_v if f else mixl_v)[p, q]

    loads[0].wait()
    loads[1].wait()
    for copy in loads[2:]:
        copy.start()
    partial_start(0, x_v[...], None)
    pl.semaphore_wait(barrier, len(near))
    copies = partial_send(0)
    for k in range(1, nz):
        pl.semaphore_signal(hello, inc=1, device_id={"lat": at_z(k) * 2 + core},
                            device_id_type=MESH)

    loads[2].wait()
    loads[3].wait()
    ku_v[...] = kd_v[...].T
    xt_v[...] = x_v[...].T
    wt_v[...] = w_v[...].T
    loads[4].wait()
    loads[5].wait()
    loads[6].wait()

    coarse = partial_done(0, copies).astype(BF16).astype(F32)
    mixed = jnp.dot(picked(coarse, 0), mixer(0), preferred_element_type=F32)
    for r in range(1, 8):
        mixed = mixed + jnp.dot(picked(coarse, r), mixer(r), preferred_element_type=F32)
    copies = spread(0, mixed)
    spread_done(0, copies)

    bacc_v[...] = jnp.zeros_like(bacc_v)
    chunk = 256

    def gate_half(h):
        lane = pl.ds(pl.multiple_of(h * 128, 128), 128)

        def gate(i, carry):
            rows = pl.ds(pl.multiple_of(i * chunk, chunk), chunk)
            pre = jnp.dot(ku_v[rows, :], mm_v[:, lane], preferred_element_type=F32)
            pre = pre + jnp.dot(ku_v[rows, :128], ml_v[:, lane], preferred_element_type=F32)
            pre = pre + jnp.dot(x_v[rows, :], w_v[:, lane], preferred_element_type=F32)
            pre = pre + bias_v[:, lane]
            cdf = 0.5 * (1.0 + lax.erf(pre * (1.0 / math.sqrt(2.0))))
            pdf = jnp.exp(-0.5 * pre * pre) * (1.0 / math.sqrt(2.0 * math.pi))
            grad = cot_v[rows, lane].astype(F32) * (cdf + pre * pdf)
            high = grad.astype(BF16)
            ghi_v[rows, lane] = high
            glo_v[rows, lane] = (grad - high.astype(F32)).astype(BF16)
            bacc_v[:, lane] += jnp.sum(grad.reshape(chunk // 8, 8, 128), axis=0)
            return carry

        lax.fori_loop(0, 1024 // chunk, gate, 0)
        total = jnp.dot(xt_v[...], ghi_v[:, lane], preferred_element_type=F32)
        cs_v[h] = total.reshape(nx, nz, tz, 8, 128)

    gate_half(1 - core)
    sem = iter(range(r_send.shape[0]))

    def send(src, dst, device):
        k = next(sem)
        return push(src, dst, r_send.at[k], r_recv.at[k], device)

    z_order = sorted(range(nz), key=lambda k: -min(k, nz - k))
    x_order = sorted(range(1, nx), key=lambda k: -min(k, nx - k))
    y_order = sorted(range(1, ny), key=lambda k: -min(k, ny - k))
    core_copies = [
        send(cs_v.at[1 - core, :, at_z(k)], cr_v.at[:, at_z(k)], partner) for k in z_order
    ]
    gate_half(core)
    bias_sum = jnp.sum(bacc_v[...], axis=0, keepdims=True)
    bs_v[0, 0:1] = bias_sum[:, :128]
    bs_v[0, 1:2] = bias_sum[:, 128:]
    bias_core = send(bs_v.at[0], bc_v, partner)


    pl.semaphore_wait(hello, nz - 1)
    own_copies = []
    for n, k in enumerate(z_order):
        core_copies[n].wait_recv()
        zi = at_z(k)
        for j in x_order + [0]:
            xi = at_x(j)
            part = cs_v[core, xi, zi] + cr_v[xi, zi]
            if j == 0 and k == 0:
                rr_v[x, z] = part
            else:
                xs_v[j, k] = part
                own_copies.append(send(xs_v.at[j, k], rr_v.at[x, z], (zi * 2 + core, xi * ny + y)))

    partial_start(1, ghi_v[...], glo_v[...])
    copies = partial_send(1)

    def bias_spread(i, order, slot, device):
        bs_v[i] = bias_part
        br_v[i, slot] = bias_part
        return [send(bs_v.at[i], br_v.at[i, slot], device(k)) for k in order]

    def bias_add(i, count, waits):
        for copy in waits:
            copy.wait_recv()
        whole = br_v[i, 0]
        for j in range(1, count):
            whole = whole + br_v[i, j]
        return whole

    bias_core.wait_recv()
    bias_part = bs_v[0] + bc_v[...]
    bias_waits = bias_spread(1, x_order, x, lambda k: {"lon": at_x(k) * ny + y})

    for copy in own_copies:
        copy.wait_recv()
    columns = []
    for i in range(nx):
        red = rr_v[i, 0]
        for j in range(1, nz):
            red = red + rr_v[i, j]
        columns.append(red)
    red = columns[0]
    for column in columns[1:]:
        red = red + column
    ys_v[...] = red
    yr_v[y] = red
    y_copies = [send(ys_v, yr_v.at[y], {"lon": x * ny + at_y(k)}) for k in y_order]
    back = partial_done(1, copies)
    bias_part = bias_add(1, nx, bias_waits)
    bias_waits = bias_spread(2, z_order[:-1], z, lambda k: {"lat": at_z(k) * 2 + core})
    back_rounded = back.astype(BF16).astype(F32)
    pull = None
    for r in range(8):
        term = lax.dot_general(picked(back_rounded, r), mixer(r), (((1,), (1,)), ((), ())),
                               preferred_element_type=F32)
        pull = term if pull is None else pull + term
    copies = spread(1, pull)

    columns = coarse.T
    for r in range(8):
        p, q, f = r // 4, (r // 2) % 2, r % 2
        outer = (columns[:, r : r + 1] * back[r : r + 1, :]).astype(BF16)
        (mhg_v if f else mlg_v)[p, q] = outer

    for copy in y_copies:
        copy.wait_recv()
    red = yr_v[0]
    for j in range(1, ny):
        red = red + yr_v[j]
    af_v[core, x, z] = red * (1.0 / math.sqrt(ncells))

    late = [k for k in z_order if min(k, nz - k) > 2 or k == z_order[0]]
    tile = af_v.at[core, x, z]
    arrivals = [
        send(tile, tile, (at_z(k) * 2 + 1 - core, at_x(j) * ny + y))
        for k in late for j in x_order + [0]
    ]
    x_copies = {}
    for k in z_order:
        x_copies[k] = [
            send(tile, tile, (at_z(k) * 2 + core, at_x(j) * ny + y))
            for j in x_order + [0] if (j, k) != (0, 0)
        ]

    bias_part = bias_add(2, nz, bias_waits)
    bias_waits = bias_spread(3, y_order, y, lambda k: {"lon": x * ny + at_y(k)})

    spread_done(1, copies)

    def back_out(i, carry):
        rows = pl.ds(pl.multiple_of(i * chunk, chunk), chunk)
        out = jnp.dot(ku_v[rows, :], mm_v[...], preferred_element_type=F32)
        out = out + jnp.dot(ku_v[rows, :128], ml_v[...], preferred_element_type=F32)
        out = out + jnp.dot(ghi_v[rows, :], wt_v[...], preferred_element_type=F32)
        fg_v[rows, :] = out.astype(BF16)
        return carry

    lax.fori_loop(0, 1024 // chunk, back_out, 0)

    for k in reversed(z_order[len(late):]):
        for copy in x_copies[k]:
            copy.wait_recv()
        column = af_v.at[core, :, lax.rem(z - k + nz, nz)]
        arrivals.append(send(column, column, partner))
    bg_v[...] = bias_add(3, ny, bias_waits) * (1.0 / math.sqrt(ncells))
    for k in late:
        arrivals += x_copies[k]
    for copy in arrivals:
        copy.wait_recv()
    for copy in sends:
        copy.wait_send()


def leave(fg_v, mlg_v, mhg_v, af_v, bias_v, fg_hbm, mlg_hbm, mhg_hbm, wg_hbm, bg_hbm,
          wg_v, bg_v, sem):
    copies = [
        pltpu.make_async_copy(fg_v, fg_hbm, sem.at[0]),
        pltpu.make_async_copy(mlg_v, mlg_hbm, sem.at[1]),
        pltpu.make_async_copy(mhg_v, mhg_hbm, sem.at[2]),
        pltpu.make_async_copy(wg_v, wg_hbm, sem.at[3]),
        pltpu.make_async_copy(bg_v, bg_hbm, sem.at[4]),
    ]
    for copy in copies[:3]:
        copy.start()
    for h in range(2):
        wg_v[:, h * 128 : (h + 1) * 128] = af_v[h].reshape(256, 128)
        bg_v[:, h * 128 : (h + 1) * 128] = bias_v[h : h + 1]
    for copy in copies[3:]:
        copy.start()
    for copy in copies:
        copy.wait()


def shards(fields, cotangent, mix_low, mix_high, point_weight, point_bias):
    nlat, nlon = lax.axis_size("lat"), lax.axis_size("lon")
    rows, cols, channels = fields.shape
    cells = rows * cols
    tables = jnp.asarray(band_tables(rows * nlat, cols * nlon, rows, cols))
    nz, ny = nlat // 2, min(ROW, nlon // 2)
    nx = nlon // ny
    tx = 32 // nx
    tz = tx // nz
    messages = 2 * (nx * nz - 1) + 3 * nx + 2 * nz + (nx - 1) + (nz - 1) + 2 * (ny - 1)
    vmem = pltpu.VMEM
    scratch = [
        vmem((cells, channels), BF16), vmem((cells, channels), BF16),
        vmem(mix_low.shape, BF16), vmem(mix_high.shape, BF16),
        vmem((channels, channels), BF16), vmem((1, channels), F32), vmem((256, cells), BF16),
        vmem((cells, 256), BF16), vmem((channels, cells), BF16), vmem((channels, channels), BF16),
        vmem((cells, channels), BF16), vmem((cells, channels), BF16),
        vmem((256, channels), BF16), vmem((128, channels), BF16), vmem((8, channels), F32),
        vmem((2, 4, 4, 8, channels), F32), vmem((2, 4, 4, 8, channels), F32),
        vmem((2, 2, 8, channels), F32), vmem((2, 4, 4, 8, channels), F32),
        vmem((2, nx, nz, tz, 8, 128), F32), vmem((nx, nz, tz, 8, 128), F32),
        vmem((nx, nz, tz, 8, 128), F32), vmem((nx, nz, tz, 8, 128), F32),
        vmem((tz, 8, 128), F32), vmem((ny, tz, 8, 128), F32),
        vmem((4, 2, 128), F32), vmem((2, 128), F32), vmem((4, max(nx, ny, nz), 2, 128), F32),
        pltpu.SemaphoreType.DMA((7,)),
        pltpu.SemaphoreType.DMA((4, 24)), pltpu.SemaphoreType.DMA((4, 24)),
        pltpu.SemaphoreType.DMA((messages,)), pltpu.SemaphoreType.DMA((messages,)),
        pltpu.SemaphoreType.REGULAR,
    ]
    outs = pl.pallas_call(
        functools.partial(kernel, (nlat, nlon, cells * nlat * nlon)),
        out_shape=(
            jax.ShapeDtypeStruct((cells, channels), BF16),
            jax.ShapeDtypeStruct(mix_low.shape, BF16),
            jax.ShapeDtypeStruct(mix_high.shape, BF16),
            jax.ShapeDtypeStruct((2, nx, nz, tz, 8, 128), F32),
            jax.ShapeDtypeStruct((2, 128), F32),
        ),
        in_specs=[pl.BlockSpec(memory_space=pltpu.HBM)] * 7,
        out_specs=[pl.BlockSpec(memory_space=vmem)] * 5,
        scratch_shapes=scratch,
        compiler_params=pltpu.CompilerParams(
            collective_id=0, has_side_effects=True, vmem_limit_bytes=32 * 1024 * 1024
        ),
        name="wavelet_block",
    )(*[
        pltpu.with_memory_space_constraint(array, pltpu.HBM)
        for array in (
            fields.reshape(cells, channels), cotangent.reshape(cells, channels), mix_low, mix_high,
            point_weight, point_bias.reshape(1, channels), tables,
        )
    ])
    outs = pl.pallas_call(
        leave,
        out_shape=(
            jax.ShapeDtypeStruct((cells, channels), BF16),
            jax.ShapeDtypeStruct(mix_low.shape, BF16),
            jax.ShapeDtypeStruct(mix_high.shape, BF16),
            jax.ShapeDtypeStruct((channels, channels), F32),
            jax.ShapeDtypeStruct((1, channels), F32),
        ),
        in_specs=[pl.BlockSpec(memory_space=vmem)] * 5,
        out_specs=[pl.BlockSpec(memory_space=pltpu.HBM)] * 5,
        scratch_shapes=[
            vmem((channels, channels), F32), vmem((1, channels), F32),
            pltpu.SemaphoreType.DMA((5,)),
        ],
        compiler_params=pltpu.CompilerParams(vmem_limit_bytes=16 * 1024 * 1024),
        name="leave",
    )(outs[0], outs[1], outs[2], outs[3].reshape(2, 32, 8, 128), outs[4])
    return (
        outs[0].reshape(fields.shape), outs[1], outs[2], outs[3], outs[4].reshape(channels),
    )


def solution(mesh):
    placed = (
        P("lat", "lon", None),
        P("lat", "lon", None),
        P("lat", "lon", None, None),
        P("lat", "lon", None, None),
        P(),
        P(),
    )
    return jax.shard_map(
        shards,
        mesh=mesh,
        in_specs=placed,
        out_specs=(
            P("lat", "lon", None),
            P("lat", "lon", None, None),
            P("lat", "lon", None, None),
            P(),
            P(),
        ),
        check_vma=False,
    )
```
